256 devices in a mesh: user: 32 (over z, y_hi, core), item: 8 (over y_lo, x).
Axes of the slice: x: 4, y: 4 (y_hi: 2, y_lo: 2; y = y_hi * 2 + y_lo), z: 8, core: 2. Of those that a mesh axis runs over, the one named last changes fastest.
Arguments:
- user_feat: bfloat16 [65536, 512], P('user'), may hold values from -6 to 6
- cotangent: bfloat16 [65536, 512], P('user'), may hold values from -6 to 6
- gain: float32 [512], replicated, may hold values from 0.25 to 1.75
- item_feat: bfloat16 [8, 2048, 512], P('item', 'user'), may hold values from -6 to 6
- categories: int32 [8, 2048], P('item', 'user'), may hold values from 0 to 31, as said below
- expert_w: bfloat16 [32, 512, 512], P('item'), may hold values from -0.25 to 0.25
- tile_place: int32 [32, 8, 80], P('user', 'item'), may hold values from 0 to 255, as said below
- tile_level: int32 [32, 8, 80, 128, 128], P('user', 'item'), may hold values from 0 to 15
- tile_count: int32 [32, 8], P('user', 'item'), may hold values from 1 to 80, as said below
Outputs:
- user_grad: bfloat16 [65536, 512], P('user', 'item')
- item_grad: bfloat16 [8, 2048, 512], P('item', 'user')
- expert_grad: float32 [32, 512, 512], P('item', 'user')
- gain_grad: float32 [512], P('item')
The draws below stay inside these ranges and needn't reach their ends.
Inputs may be any that keep to these rules, and one draw needn't show every extreme that they name: The categories of items of item shard j lie in j * 4 to (j + 1) * 4 - 1. `tile_place`: within one device the 80 slots name distinct positions. `tile_count`: slots at or past the count are unused; some device has all 80 slots live.
All inputs are finite; a program needn't handle non-finite values.
Results may differ from the reference program's by a relative error of at most 0.0065.
Values may be sent and summed in bfloat16 or wider, within the bound.
A program may use at most 128 MiB of HBM per device.

```python
import jax
import jax.numpy as jnp
from jax import lax

D = 512
TILE = 128
EXP_SHARD = 4
UT = 16
IT = 16
NT = 80
USHARDS = 32
ISHARDS = 8
EXPERTS = 32
ITEMS_SH = 2048
NU = 65536


def draw_categories(key, part):
    picks = jax.random.randint(key, (ISHARDS, ITEMS_SH), 0, EXP_SHARD)
    return (picks + jnp.arange(ISHARDS, dtype=jnp.int32)[:, None] * EXP_SHARD).astype(jnp.int32)


def draw_tile_place(key, part):
    keys = jax.random.split(key, USHARDS * ISHARDS)
    chosen = jax.vmap(lambda one_key: jax.random.permutation(one_key, UT * IT)[:NT])(keys)
    return chosen.reshape(USHARDS, ISHARDS, NT).astype(jnp.int32)


def draw_tile_count(key, part):
    first_key, second_key = jax.random.split(key)
    devices_all = USHARDS * ISHARDS
    counts = jax.random.randint(first_key, (devices_all,), max(1, NT // 8), NT // 2 + 1)
    full_one = jax.random.randint(second_key, (), 0, devices_all)
    counts = jnp.where(jnp.arange(devices_all, dtype=jnp.int32) == full_one, NT, counts)
    return counts.reshape(USHARDS, ISHARDS).astype(jnp.int32)


def set_ends(drawn, rng, least, largest):
    longest = drawn.shape.index(max(drawn.shape))
    spots = []
    for shift in (0, 1):
        where = [jax.random.randint(jax.random.fold_in(rng, axis), (), 0, length) for axis, length in enumerate(drawn.shape)]
        where[longest] = (where[longest] + shift) % drawn.shape[longest]
        spots.append(tuple(where))
    return drawn.at[spots[0]].set(least).at[spots[1]].set(largest)


def shard_levels(key, shape, cuts, low, high):
    level, own = 1.0, jax.random.fold_in(key, 6)
    for dim, shards_of in cuts:
        steps = jnp.exp(jax.random.uniform(jax.random.fold_in(own, dim), (shards_of,), jnp.float32, low / len(cuts), high / len(cuts)))
        level = level * jnp.repeat(steps, shape[dim] // shards_of).reshape([-1 if axis == dim else 1 for axis in range(len(shape))])
    return level


def gaussian(key, shape, width, limit, cuts=(), held_as=jnp.bfloat16):
    level = shard_levels(key, shape, cuts, -0.22, 0.18) if cuts else 1.0
    result = jax.random.normal(key, shape, jnp.float32) * width * level
    return jnp.minimum(jnp.maximum(result, -limit), limit).astype(held_as)


def setup_inputs(seed: int = 0) -> dict:
    key_list = jax.random.split(jax.random.key(seed), 10)
    user_feat = gaussian(key_list[0], (NU, D), 1.0, 6.0, ((0, 32),))
    cotangent = gaussian(key_list[1], (NU, D), 1.0, 6.0, ((0, 32),))
    gain = jnp.clip(1.0 + 0.15 * jax.random.normal(key_list[2], (D,), jnp.float32), 0.25, 1.75)
    item_feat = gaussian(key_list[3], (ISHARDS, ITEMS_SH, D), 1.0, 6.0, ((0, 8), (1, 32)))
    categories = draw_categories(jax.random.fold_in(key_list[9], 71), 0)
    expert_w = gaussian(key_list[5], (EXPERTS, D, D), D ** -0.5, 0.25, ((0, 8),))
    tile_place = draw_tile_place(jax.random.fold_in(key_list[9], 71), 0)
    tile_level = set_ends(jax.random.randint(key_list[7], (USHARDS, ISHARDS, NT, TILE, TILE), 0, 16), jax.random.fold_in(key_list[7], 1), 0, 15).astype(jnp.int32)
    tile_count = draw_tile_count(jax.random.fold_in(key_list[9], 71), 0)
    return dict(user_feat=user_feat, cotangent=cotangent, gain=gain, item_feat=item_feat, categories=categories, expert_w=expert_w, tile_place=tile_place, tile_level=tile_level, tile_count=tile_count)


def tile_setup(places, levels, counts):
    live_mask = (jnp.arange(NT, dtype=jnp.int32) < counts).astype(jnp.float32)
    tile_weights = levels.astype(jnp.float32) * (1.0 / (2.0 * TILE)) * live_mask[:, None, None]
    return (tile_weights, places // IT, places % IT)

def spread_items(tile_weights, row_block, col_block, queries):
    picked = jnp.take(queries.reshape(IT, TILE, D), col_block, axis=0)
    products = jnp.einsum('sij,sjd->sid', tile_weights, picked, precision=lax.Precision.HIGHEST)
    onehot = (row_block[:, None] == jnp.arange(UT, dtype=jnp.int32)[None, :]).astype(jnp.float32)
    return jnp.einsum('su,sid->uid', onehot, products, precision=lax.Precision.HIGHEST).reshape(UT * TILE, D)

def spread_users(tile_weights, row_block, col_block, grads):
    picked = jnp.take(grads.reshape(UT, TILE, D), row_block, axis=0)
    products = jnp.einsum('sij,sid->sjd', tile_weights, picked, precision=lax.Precision.HIGHEST)
    onehot = (col_block[:, None] == jnp.arange(IT, dtype=jnp.int32)[None, :]).astype(jnp.float32)
    return jnp.einsum('sc,sjd->cjd', onehot, products, precision=lax.Precision.HIGHEST).reshape(IT * TILE, D)

def reference(user_feat, cotangent, gain, item_feat, categories, expert_w, tile_place, tile_level, tile_count):
    by_shard = expert_w.reshape(ISHARDS, EXP_SHARD, D, D)
    shard_ids = jnp.arange(ISHARDS, dtype=jnp.int32)

    def project(inputs):
        item_rows, item_cats, matrices, shard_id = inputs
        acc_total = jnp.zeros((ITEMS_SH, D), jnp.float32)
        for expert in range(EXP_SHARD):
            chosen = item_cats == shard_id * EXP_SHARD + expert
            acc_total = acc_total + jnp.where(chosen[:, None], jnp.dot(item_rows, matrices[expert], preferred_element_type=jnp.float32), 0.0)
        return acc_total.astype(jnp.bfloat16)
    queries = lax.map(project, (item_feat, categories, by_shard, shard_ids)).astype(jnp.float32)
    users = user_feat.reshape(USHARDS, UT * TILE, D)
    grads = cotangent.reshape(USHARDS, UT * TILE, D)

    def per_user(running, inputs):
        item_acc, gain_acc = running
        user_rows, grad_rows, places, levels, counts = inputs

        def add_items(acc_total, pieces):
            one_place, one_level, one_count, one_query = pieces
            tile_weights, row_block, col_block = tile_setup(one_place, one_level, one_count)
            return (acc_total + spread_items(tile_weights, row_block, col_block, one_query), None)
        summed, _ = lax.scan(add_items, jnp.zeros((UT * TILE, D), jnp.float32), (places, levels, counts, queries))
        pre_norm = user_rows.astype(jnp.float32) + summed
        inv_rms = lax.rsqrt(lax.optimization_barrier(jnp.mean(pre_norm * pre_norm, axis=-1, keepdims=True)) + 1e-05)
        grad_float = grad_rows.astype(jnp.float32)
        scaled_grad = gain[None, :] * grad_float
        cross_mean = lax.optimization_barrier(jnp.mean(scaled_grad * pre_norm, axis=-1, keepdims=True))
        state_grad = (inv_rms * scaled_grad - inv_rms ** 3 * pre_norm * cross_mean).astype(jnp.bfloat16)
        gain_acc = gain_acc + lax.optimization_barrier(jnp.sum(grad_float * pre_norm * inv_rms, axis=0))
        grad_wide = state_grad.astype(jnp.float32)

        def item_terms(pieces):
            one_place, one_level, one_count = pieces
            tile_weights, row_block, col_block = tile_setup(one_place, one_level, one_count)
            return spread_users(tile_weights, row_block, col_block, grad_wide)
        item_acc = item_acc + lax.map(item_terms, (places, levels, counts))
        return ((item_acc, gain_acc), state_grad)
    initial = (jnp.zeros((ISHARDS, ITEMS_SH, D), jnp.float32), jnp.zeros((D,), jnp.float32))
    (item_acc, gain_grad), user_blocks = lax.scan(per_user, initial, (users, grads, tile_place, tile_level, tile_count))
    user_grad = user_blocks.reshape(NU, D)
    rounded = item_acc.astype(jnp.bfloat16)

    def finish(inputs):
        item_rows, item_cats, matrices, shard_id, sums_rows = inputs
        acc_total = jnp.zeros((ITEMS_SH, D), jnp.float32)
        grad_list = []
        for expert in range(EXP_SHARD):
            chosen = item_cats == shard_id * EXP_SHARD + expert
            acc_total = acc_total + jnp.where(chosen[:, None], jnp.dot(sums_rows, matrices[expert].T, preferred_element_type=jnp.float32), 0.0)
            masked = jnp.where(chosen[:, None], item_rows, jnp.zeros_like(item_rows))
            grad_list.append(jnp.dot(masked.T, sums_rows, preferred_element_type=jnp.float32))
        return (acc_total.astype(jnp.bfloat16), jnp.stack(grad_list))
    item_grad, expert_grad = lax.map(finish, (item_feat, categories, by_shard, shard_ids, rounded))
    return (user_grad, item_grad, expert_grad.reshape(EXPERTS, D, D), gain_grad)
```

```python
import jax
import jax.numpy as jnp
from jax import lax
from jax.experimental import pallas as pl
from jax.experimental.pallas import tpu as pltpu
from jax.sharding import PartitionSpec as P

MESH = pl.DeviceIdType.MESH
F32 = jnp.float32
BF16 = jnp.bfloat16
DMA = pltpu.SemaphoreType.DMA
R, L = 0, 1
DIR = (1, -1)


def layer(
    x_ref, cat_ref, gain_ref, inv_ref, scale_ref, w_hbm, lvl_hbm, uf_hbm, ct_hbm,
    ug_out, ig_out, eg_out, gg_out,
    xg, w, lvl, amat, q, acc, uf, ct, catr, catl,
    mxs, mxr, mys, myr, ugall, ugt, acc2,
    cs, cr, rs, rr, ys, yr, sumb, st, ms, es, er, igt, gs, gr, gt, gr2,
    sem_loc, sem_cs, sem_cr, sem_ays, sem_ayr, sem_azs, sem_azr, sem_acs, sem_acr,
    sem_ixs, sem_ixr, sem_iys, sem_iyr, sem_gxs, sem_gxr, sem_gys, sem_gyr,
    sem_ucs, sem_ucr, sem_uzs, sem_uzr, sem_uys, sem_uyr,
    sem_1s, sem_1r, sem_2s, sem_2r, sem_g1s, sem_g1r, sem_g2s, sem_g2r,
):
    u = lax.axis_index("user")
    j = lax.axis_index("item")
    z, yh, c = u // 4, (u // 2) % 2, u % 2
    yl, x = j // 4, j % 4

    def at_z(d):
        return (((z + d + 8) % 8) * 4 + yh * 2 + c, j)

    def at_x(d):
        return (u, yl * 4 + (x + d + 4) % 4)

    y_user = (z * 4 + (1 - yh) * 2 + c, j)
    core = (z * 4 + yh * 2 + 1 - c, j)
    y_item = (u, (1 - yl) * 4 + x)

    def peer_u(k):
        return ((u + k) % 32, j)

    def peer_i(k):
        return (u, ((yl + k // 4) % 2) * 4 + (x + k % 4) % 4)

    sent = []

    def remote(src, dst, ssem, rsem, dev):
        return pltpu.make_async_remote_copy(
            src_ref=src, dst_ref=dst, send_sem=ssem, recv_sem=rsem, device_id=dev, device_id_type=MESH
        )

    def send(src, dst, ssem, rsem, dev):
        copy = remote(src, dst, ssem, rsem, dev)
        copy.start()
        sent.append(copy)

    def recv(dst, ssem, rsem, dev):
        remote(dst, dst, ssem, rsem, dev).wait_recv()

    rows = pl.ds(pl.multiple_of(j * 256, 256), 256)
    local = [
        pltpu.make_async_copy(lvl_hbm, lvl, sem_loc.at[0]),
        pltpu.make_async_copy(w_hbm, w, sem_loc.at[1]),
        pltpu.make_async_copy(uf_hbm.at[rows], uf, sem_loc.at[2]),
        pltpu.make_async_copy(ct_hbm.at[rows], ct, sem_loc.at[3]),
    ]
    for copy in local:
        copy.start()
    xg[z, yh * 2 + c] = x_ref[...]
    catr[u] = cat_ref[...]

    barrier = pltpu.get_barrier_semaphore()

    def greet_u(k, _):
        pl.semaphore_signal(barrier, inc=1, device_id=peer_u(k), device_id_type=MESH)
        return 0

    def greet_i(k, _):
        pl.semaphore_signal(barrier, inc=1, device_id=peer_i(k), device_id_type=MESH)
        return 0

    lax.fori_loop(1, 32, greet_u, 0)
    lax.fori_loop(1, 8, greet_i, 0)
    pl.semaphore_wait(barrier, 38)

    own = xg.at[z, yh * 2 + c]
    send(own, own, sem_ays.at[0], sem_ayr.at[0], y_user)
    for d in (R, L):
        send(own, own, sem_azs.at[d, 0, 0], sem_azr.at[d, 0, 0], at_z(DIR[d]))
    send(own, own, sem_acs.at[0, 0], sem_acr.at[0, 0], core)

    def cats_start(k, _):
        remote(catr.at[u], catr.at[u], sem_cs.at[k], sem_cr.at[k], peer_u(k)).start()
        return 0

    lax.fori_loop(1, 32, cats_start, 0)

    def build(d):
        zs = (z + d + 8) % 8

        def body(rb, _):
            for half in range(2):
                pos = rb * 16 + zs * 2 + half
                tile = lvl[inv_ref[pos]].astype(F32) * scale_ref[pos]
                amat[zs, pl.ds(pl.multiple_of(rb * 128, 128), 128), half * 128 : half * 128 + 128] = tile.astype(BF16)
            return 0

        lax.fori_loop(0, 16, body, 0)

    def hops(d, k):
        return 4 if (k == 0) == (d == R) else 3

    def gather_step(s):
        for k in range(2):
            for d in (R, L):
                if s > hops(d, k):
                    continue
                zs = (z - DIR[d] * s + 8) % 8
                block = xg.at[zs, (yh if k == 0 else 1 - yh) * 2 + c]
                recv(block, sem_azs.at[d, k, s - 1], sem_azr.at[d, k, s - 1], at_z(-DIR[d]))
                if s < hops(d, k):
                    send(block, block, sem_azs.at[d, k, s], sem_azr.at[d, k, s], at_z(DIR[d]))
                slot = s * 2 + d if s < 4 else 8
                slot = (s if d == R else 8 - s) % 8
                send(block, block, sem_acs.at[slot, k], sem_acr.at[slot, k], core)

    def project(d, first):
        zs = (z + d + 8) % 8
        slot = (-d) % 8
        for k in range(2):
            block = xg.at[zs, (yh if k == 0 else 1 - yh) * 2 + 1 - c]
            recv(block, sem_acs.at[slot, k], sem_acr.at[slot, k], core)
        feats = xg[zs].reshape(256, 512).astype(F32)
        col = jnp.concatenate(
            [jnp.transpose(catl[zs * 2 + half])[:, 0:1] for half in range(2)], axis=0
        )
        total = jnp.zeros((256, 512), F32)
        for expert in range(4):
            masked = jnp.where(col == float(expert), feats, 0.0).astype(BF16)
            total = total + jnp.dot(masked, w[expert], preferred_element_type=F32)
        q[...] = total.astype(BF16)

        def body(r, _):
            part = jnp.dot(
                amat[zs, pl.ds(pl.multiple_of(r * 256, 256), 256), :], q[...], preferred_element_type=F32
            ).reshape(2, 128, 512)
            acc[pl.ds(r * 2, 2)] = part if first else acc[pl.ds(r * 2, 2)] + part
            return 0

        lax.fori_loop(0, 8, body, 0)

    local[0].wait()
    build(0)
    block = xg.at[z, (1 - yh) * 2 + c]
    recv(block, sem_ays.at[0], sem_ayr.at[0], y_user)
    for d in (R, L):
        send(block, block, sem_azs.at[d, 1, 0], sem_azr.at[d, 1, 0], at_z(DIR[d]))
    send(block, block, sem_acs.at[0, 1], sem_acr.at[0, 1], core)
    build(1)
    gather_step(1)
    local[1].wait()

    def cats_wait(k, _):
        src = catr.at[(u + 32 - k) % 32]
        remote(src, src, sem_cs.at[k], sem_cr.at[k], peer_u(k)).wait()
        return 0

    lax.fori_loop(1, 32, cats_wait, 0)
    low = lax.broadcasted_iota(jnp.int32, (8, 128), 1) < 64

    def cats_pair(p, _):
        catl[p] = jnp.where(low, catr[p * 2], catr[p * 2 + 1])
        return 0

    lax.fori_loop(0, 16, cats_pair, 0)
    project(0, True)
    build(-1)
    gather_step(2)
    project(1, False)
    project(-1, False)
    build(2)
    gather_step(3)
    build(-2)
    project(2, False)
    project(-2, False)
    build(3)
    gather_step(4)
    build(-3)
    project(3, False)
    project(-3, False)
    build(4)
    project(4, False)

    local[2].wait()
    local[3].wait()

    def ihops(d, h):
        return 2 if (h == 0) == (d == R) else 1

    def chunk(dx, y, h):
        return (y * 4 + (x + dx + 4) % 4) * 2 + h

    def ysel(k):
        return 1 - yl if k == 0 else yl

    def mx_send(d, k, h, s, value):
        mxs[d, k, h, s] = value.astype(BF16)
        send(mxs.at[d, k, h, s], mxr.at[d, k, h, s], sem_ixs.at[d, k, h, s], sem_ixr.at[d, k, h, s], at_x(DIR[d]))

    def mx_recv(d, k, h, s):
        recv(mxr.at[d, k, h, s], sem_ixs.at[d, k, h, s], sem_ixr.at[d, k, h, s], at_x(-DIR[d]))
        return mxr[d, k, h, s].astype(F32)

    combos = [(k, d, h) for k in range(2) for d in (R, L) for h in range(2)]
    for k, d, h in combos:
        if ihops(d, h) == 2:
            mx_send(d, k, h, 1, acc[chunk(2 * DIR[d], ysel(k), h)])
    for k, d, h in combos:
        if ihops(d, h) == 1:
            mx_send(d, k, h, 0, acc[chunk(DIR[d], ysel(k), h)])
    for k, d, h in combos:
        if ihops(d, h) == 2:
            part = mx_recv(d, k, h, 1)
            mx_send(d, k, h, 0, acc[chunk(DIR[d], ysel(k), h)] + part)
    for h in range(2):
        value = acc[chunk(0, 1 - yl, h)] + mx_recv(R, 0, h, 0) + mx_recv(L, 0, h, 0)
        mys[h] = value.astype(BF16)
        send(mys.at[h], myr.at[h], sem_iys.at[h], sem_iyr.at[h], y_item)

    gain = gain_ref[...]
    gsum = jnp.zeros((1, 512), F32)
    for h in range(2):
        value = acc[chunk(0, yl, h)] + mx_recv(R, 1, h, 0) + mx_recv(L, 1, h, 0)
        recv(myr.at[h], sem_iys.at[h], sem_iyr.at[h], y_item)
        pre = uf[h * 128 : h * 128 + 128, :].astype(F32) + value + myr[h].astype(F32)
        grad = ct[h * 128 : h * 128 + 128, :].astype(F32)
        scaled = gain * grad
        inv = lax.rsqrt(jnp.sum(pre * pre, axis=-1, keepdims=True) * (1.0 / 512) + 1e-05)
        cross = jnp.sum(scaled * pre, axis=-1, keepdims=True) * (1.0 / 512)
        ugall[j, h] = (inv * scaled - inv * inv * inv * pre * cross).astype(BF16)
        gsum = gsum + jnp.sum(grad * pre * inv, axis=0, keepdims=True)
        mine = ugall.at[j, h]
        send(mine, mine, sem_gys.at[h], sem_gyr.at[h], y_item)
        for d in (R, L):
            send(mine, mine, sem_gxs.at[d, 0, h, 0], sem_gxr.at[d, 0, h, 0], at_x(DIR[d]))
    gs[...] = jnp.zeros((8, 128), F32)
    for t in range(4):
        gs[t : t + 1, :] = gsum[:, t * 128 : t * 128 + 128]

    def gain_i(k, _):
        remote(gs, gr.at[k], sem_g1s.at[k], sem_g1r.at[k], peer_i(k)).start()
        return 0

    lax.fori_loop(1, 8, gain_i, 0)

    def back(jj, first):
        ugt[...] = jnp.transpose(ugall[jj].reshape(256, 512).astype(F32)).astype(BF16)

        def body(zs, _):
            part = jnp.dot(
                ugt[...],
                amat[zs, pl.ds(pl.multiple_of(jj * 256, 256), 256), :],
                preferred_element_type=F32,
            )
            acc2[zs] = part if first else acc2[zs] + part
            return 0

        lax.fori_loop(0, 8, body, 0)

    def jat(dx, y):
        return y * 4 + (x + dx + 4) % 4

    def g_step(k, s):
        y = yl if k == 0 else 1 - yl
        for h in range(2):
            for d in (R, L):
                if s > ihops(d, h):
                    continue
                block = ugall.at[jat(-DIR[d] * s, y), h]
                recv(block, sem_gxs.at[d, k, h, s - 1], sem_gxr.at[d, k, h, s - 1], at_x(-DIR[d]))
                if s < ihops(d, h):
                    send(block, block, sem_gxs.at[d, k, h, s], sem_gxr.at[d, k, h, s], at_x(DIR[d]))

    for h in range(2):
        other = ugall.at[jat(0, 1 - yl), h]
        recv(other, sem_gys.at[h], sem_gyr.at[h], y_item)
        for d in (R, L):
            send(other, other, sem_gxs.at[d, 1, h, 0], sem_gxr.at[d, 1, h, 0], at_x(DIR[d]))
    back(j, True)
    g_step(0, 1)
    back(jat(0, 1 - yl), False)
    back(jat(1, yl), False)
    g_step(1, 1)
    back(jat(-1, yl), False)
    back(jat(1, 1 - yl), False)
    g_step(0, 2)
    back(jat(-1, 1 - yl), False)
    back(jat(2, yl), False)
    g_step(1, 2)
    back(jat(2, 1 - yl), False)

    def gain_i_wait(k, total):
        remote(gs, gr.at[k], sem_g1s.at[k], sem_g1r.at[k], peer_i(k)).wait()
        return total + gr[k]

    gt[...] = lax.fori_loop(1, 8, gain_i_wait, gs[...])

    def gain_u(k, _):
        remote(gt, gr2.at[k], sem_g2s.at[k], sem_g2r.at[k], peer_u(k)).start()
        return 0

    def urows(zs, y, cc):
        return pl.ds(pl.multiple_of((zs * 4 + y * 2 + cc) * 16, 16), 16)

    order = (4, 3, -3, 2, -2, 1, -1, 0)
    for d in order:
        zs = (z + d + 8) % 8
        for y in range(2):
            cs[zs, y] = acc2[:, urows(zs, y, 1 - c), :].astype(BF16)
        send(cs.at[zs], cr.at[zs], sem_ucs.at[d % 8], sem_ucr.at[d % 8], core)
    lax.fori_loop(1, 32, gain_u, 0)

    def core_recv(d):
        zs = (z + d + 8) % 8
        recv(cr.at[zs], sem_ucs.at[d % 8], sem_ucr.at[d % 8], core)

    def own_sum(d, y):
        zs = (z + d + 8) % 8
        return acc2[:, urows(zs, y, c), :] + cr[zs, y].astype(F32)

    def z_send(d, k, s, value):
        rs[d, k, s] = value.astype(BF16)
        send(rs.at[d, k, s], rr.at[d, k, s], sem_uzs.at[d, k, s], sem_uzr.at[d, k, s], at_z(DIR[d]))

    def z_recv(d, k, s):
        recv(rr.at[d, k, s], sem_uzs.at[d, k, s], sem_uzr.at[d, k, s], at_z(-DIR[d]))
        return rr[d, k, s].astype(F32)

    def uy(k):
        return 1 - yh if k == 0 else yh

    ucombos = [(k, d) for k in range(2) for d in (R, L)]
    for s in (4, 3, 2, 1):
        if s == 4:
            core_recv(4)
        else:
            core_recv(s)
            core_recv(-s)
        for k, d in ucombos:
            if hops(d, k) == s:
                z_send(d, k, s - 1, own_sum(DIR[d] * s, uy(k)))
        for k, d in ucombos:
            if hops(d, k) > s:
                z_send(d, k, s - 1, own_sum(DIR[d] * s, uy(k)) + z_recv(d, k, s))
    core_recv(0)
    ys[...] = (own_sum(0, 1 - yh) + z_recv(R, 0, 0) + z_recv(L, 0, 0)).astype(BF16)
    send(ys, yr, sem_uys.at[0], sem_uyr.at[0], y_user)
    mine = own_sum(0, yh) + z_recv(R, 1, 0) + z_recv(L, 1, 0)
    recv(yr, sem_uys.at[0], sem_uyr.at[0], y_user)
    mine = (mine + yr[...].astype(F32)).astype(BF16)
    for zs in range(8):
        for half in range(2):
            sumb[zs * 2 + half] = mine[zs, :, half * 128 : half * 128 + 128]

    st[u] = sumb[u // 2]

    def sums_start(k, _):
        remote(sumb.at[((u + k) % 32) // 2], st.at[u], sem_1s.at[k], sem_1r.at[k], peer_u(k)).start()
        return 0

    lax.fori_loop(1, 32, sums_start, 0)

    for p in range(16):
        cat16 = jnp.concatenate([catl[p], catl[p]], axis=0)
        value = sumb[p].astype(F32)
        for expert in range(4):
            ms[expert * 16 : expert * 16 + 16, p * 128 : p * 128 + 128] = jnp.where(
                cat16 == float(expert), value, 0.0
            ).astype(BF16)
    grads = jnp.zeros((64, 512), F32)
    for zs in range(8):
        grads = grads + jnp.dot(
            ms[:, zs * 256 : zs * 256 + 256], xg[zs].reshape(256, 512), preferred_element_type=F32
        )
    wide = jnp.transpose(jnp.concatenate([grads, grads], axis=0)).reshape(32, 16, 128)
    es[...] = wide
    er[u] = es[u]

    def grads_start(k, _):
        remote(es.at[(u + k) % 32], er.at[u], sem_2s.at[k], sem_2r.at[k], peer_u(k)).start()
        return 0

    lax.fori_loop(1, 32, grads_start, 0)

    def gain_u_wait(k, total):
        remote(gt, gr2.at[k], sem_g2s.at[k], sem_g2r.at[k], peer_u(k)).wait()
        return total + gr2[k]

    gs2 = lax.fori_loop(1, 32, gain_u_wait, gt[...])
    gr[0] = gs2
    grow = gr[0, pl.ds(j // 2, 1), :]
    gg_out[...] = jnp.where(j % 2 == 0, grow[:, 0:64], grow[:, 64:128])

    def own_cols(jj, _):
        for h in range(2):
            wide = ugall[jj, h, :, pl.ds(pl.multiple_of((j // 2) * 128, 128), 128)]
            ug_out[pl.ds(pl.multiple_of(jj * 256 + h * 128, 128), 128), :] = jnp.where(
                j % 2 == 0, wide[:, 0:64], wide[:, 64:128]
            )
        return 0

    lax.fori_loop(0, 8, own_cols, 0)

    def sums_wait(k, _):
        dst = st.at[(u + 32 - k) % 32]
        remote(dst, dst, sem_1s.at[k], sem_1r.at[k], peer_u(k)).wait()
        return 0

    lax.fori_loop(1, 32, sums_wait, 0)
    sums = st[...].reshape(512, 128).astype(F32)
    cat1 = catl[u // 2][0:1, :]
    total = jnp.zeros((512, 128), F32)
    for expert in range(4):
        masked = jnp.where(cat1 == float(expert), sums, 0.0).astype(BF16)
        total = total + jnp.dot(w[expert], masked, preferred_element_type=F32)
    igt[...] = jnp.transpose(total)
    ig_out[...] = igt[pl.ds(pl.multiple_of(c * 64, 64), 64), :].astype(BF16)

    def grads_wait(k, _):
        dst = er.at[(u + 32 - k) % 32]
        remote(dst, dst, sem_2s.at[k], sem_2r.at[k], peer_u(k)).wait()
        return 0

    lax.fori_loop(1, 32, grads_wait, 0)
    lane = lax.broadcasted_iota(jnp.int32, (16, 128), 1) // 16
    for expert in range(4):
        for t in range(4):
            line = jnp.zeros((16, 128), F32)
            for k in range(8):
                moved = pltpu.roll(er[t * 8 + k], (k * 16 - expert * 16) % 128, 1)
                line = jnp.where(lane == k, moved, line)
            eg_out[expert, :, t * 128 : t * 128 + 128] = line

    for copy in sent:
        copy.wait_send()


def on_device(
    user_feat, cotangent, gain, item_feat, categories, expert_w, tile_place, tile_level, tile_count
):
    first_cat = lax.axis_index("item") * 4
    cats = (categories[0] - first_cat).astype(F32)
    cats = jnp.broadcast_to(jnp.concatenate([cats, cats])[None, :], (8, 128))
    place = tile_place[0, 0]
    live = jnp.arange(80, dtype=jnp.int32) < tile_count[0, 0]
    hit = (place[None, :] == jnp.arange(256, dtype=jnp.int32)[:, None]) & live[None, :]
    inv = jnp.sum(jnp.where(hit, jnp.arange(80, dtype=jnp.int32)[None, :], 0), axis=1)
    scale = jnp.where(jnp.any(hit, axis=1), 1.0 / 256, 0.0).astype(F32)

    vmem = pl.BlockSpec(memory_space=pltpu.VMEM)
    smem = pl.BlockSpec(memory_space=pltpu.SMEM)
    hbm = pl.BlockSpec(memory_space=pl.ANY)
    V = pltpu.VMEM
    scratch = [
        V((8, 4, 64, 512), BF16), V((4, 512, 512), BF16), V((80, 128, 128), jnp.int32),
        V((8, 2048, 256), BF16), V((256, 512), BF16), V((16, 128, 512), F32),
        V((256, 512), BF16), V((256, 512), BF16), V((32, 8, 128), F32), V((16, 8, 128), F32),
        V((2, 2, 2, 2, 128, 512), BF16), V((2, 2, 2, 2, 128, 512), BF16),
        V((2, 128, 512), BF16), V((2, 128, 512), BF16),
        V((8, 2, 128, 512), BF16), V((512, 256), BF16), V((8, 512, 256), F32),
        V((8, 2, 8, 16, 256), BF16), V((8, 2, 8, 16, 256), BF16),
        V((2, 2, 4, 8, 16, 256), BF16), V((2, 2, 4, 8, 16, 256), BF16),
        V((8, 16, 256), BF16), V((8, 16, 256), BF16),
        V((16, 16, 128), BF16), V((32, 16, 128), BF16), V((64, 2048), BF16),
        V((32, 16, 128), F32), V((32, 16, 128), F32), V((128, 512), F32),
        V((8, 128), F32), V((8, 8, 128), F32), V((8, 128), F32), V((32, 8, 128), F32),
        DMA((4,)), DMA((32,)), DMA((32,)), DMA((1,)), DMA((1,)), DMA((2, 2, 4)), DMA((2, 2, 4)),
        DMA((8, 2)), DMA((8, 2)),
        DMA((2, 2, 2, 2)), DMA((2, 2, 2, 2)), DMA((2,)), DMA((2,)),
        DMA((2, 2, 2, 2)), DMA((2, 2, 2, 2)), DMA((2,)), DMA((2,)),
        DMA((8,)), DMA((8,)), DMA((2, 2, 4)), DMA((2, 2, 4)), DMA((1,)), DMA((1,)),
        DMA((32,)), DMA((32,)), DMA((32,)), DMA((32,)), DMA((8,)), DMA((8,)), DMA((32,)), DMA((32,)),
    ]
    ug, ig, eg, gg = pl.pallas_call(
        layer,
        out_shape=(
            jax.ShapeDtypeStruct((2048, 64), BF16),
            jax.ShapeDtypeStruct((64, 512), BF16),
            jax.ShapeDtypeStruct((4, 16, 512), F32),
            jax.ShapeDtypeStruct((1, 64), F32),
        ),
        in_specs=[vmem, vmem, vmem, smem, smem, hbm, hbm, hbm, hbm],
        out_specs=(vmem, vmem, vmem, vmem),
        scratch_shapes=scratch,
        compiler_params=pltpu.CompilerParams(
            collective_id=0, has_side_effects=True, vmem_limit_bytes=60 * 2**20
        ),
    )(
        item_feat[0], cats, gain[None, :], inv, scale, expert_w, tile_level[0, 0], user_feat, cotangent
    )
    return ug, ig[None], eg, gg[0]


def solution(mesh):
    placed = (
        P("user", None),
        P("user", None),
        P(),
        P("item", "user", None),
        P("item", "user"),
        P("item", None, None),
        P("user", "item", None),
        P("user", "item", None, None, None),
        P("user", "item"),
    )
    return jax.shard_map(
        on_device,
        mesh=mesh,
        in_specs=placed,
        out_specs=(P("user", "item"), P("item", "user", None), P("item", "user", None), P("item")),
        check_vma=False,
    )
```

```python
import jax
import jax.numpy as jnp
from jax import lax
from jax.experimental import pallas as pl
from jax.experimental.pallas import tpu as pltpu
from jax.sharding import PartitionSpec as P

MESH = pl.DeviceIdType.MESH
F32 = jnp.float32
BF16 = jnp.bfloat16
DMA = pltpu.SemaphoreType.DMA
R, L = 0, 1
DIR = (1, -1)


def layer(
    x_ref, cat_ref, gain_ref, place_ref, count_ref, w_hbm, lvl_hbm, uf_hbm, ct_hbm,
    ug_out, ig_out, eg_out, gg_out,
    xg, qg, w, lvl, amat, acc, uf, ct, catr, catl, tab, tabs,
    mxs, mxr, mys, myr, ugall, ugt, acc2,
    cs, cr, rs, rr, ys, yr, sumb, st, ms, es, er, igt, gs, gr, gt, gr2,
    sem_loc, sem_cs, sem_cr, sem_q, sem_f,
    sem_ixs, sem_ixr, sem_iys, sem_iyr, sem_gxs, sem_gxr, sem_gys, sem_gyr,
    sem_ucs, sem_ucr, sem_uzs, sem_uzr, sem_uys, sem_uyr,
    sem_1s, sem_1r, sem_2s, sem_2r, sem_g1s, sem_g1r, sem_g2s, sem_g2r,
):
    u = lax.axis_index("user")
    j = lax.axis_index("item")
    z, yh, c = u // 4, (u // 2) % 2, u % 2
    yl, x = j // 4, j % 4

    def at_z(d):
        return (((z + d + 8) % 8) * 4 + yh * 2 + c, j)

    def at_x(d):
        return (u, yl * 4 + (x + d + 4) % 4)

    y_user = (z * 4 + (1 - yh) * 2 + c, j)
    core = (z * 4 + yh * 2 + 1 - c, j)
    y_item = (u, (1 - yl) * 4 + x)

    def peer_u(k):
        return ((u + k) % 32, j)

    def peer_i(k):
        return (u, ((yl + k // 4) % 2) * 4 + (x + k % 4) % 4)

    sent = []

    def remote(src, dst, ssem, rsem, dev):
        return pltpu.make_async_remote_copy(
            src_ref=src, dst_ref=dst, send_sem=ssem, recv_sem=rsem, device_id=dev, device_id_type=MESH
        )

    def send(src, dst, ssem, rsem, dev):
        copy = remote(src, dst, ssem, rsem, dev)
        copy.start()
        sent.append(copy)

    def recv(dst, ssem, rsem, dev):
        remote(dst, dst, ssem, rsem, dev).wait_recv()

    barrier = pltpu.get_barrier_semaphore()
    for dev in (at_z(1), at_z(-1), at_x(1), at_x(-1), y_user, y_item, core):
        pl.semaphore_signal(barrier, inc=1, device_id=dev, device_id_type=MESH)

    rows = pl.ds(pl.multiple_of(j * 256, 256), 256)
    local = [
        pltpu.make_async_copy(w_hbm, w, sem_loc.at[1]),
        pltpu.make_async_copy(lvl_hbm, lvl, sem_loc.at[0]),
        pltpu.make_async_copy(uf_hbm.at[rows], uf, sem_loc.at[2]),
        pltpu.make_async_copy(ct_hbm.at[rows], ct, sem_loc.at[3]),
    ]
    for copy in local:
        copy.start()

    spot = lax.broadcasted_iota(jnp.int32, (8, 128), 0) * 128 + lax.broadcasted_iota(jnp.int32, (8, 128), 1)

    def place_slot(s, table):
        key = jnp.where(s < count_ref[0, 0], place_ref[s], -1)
        return jnp.where(spot == key, s, table)

    tab[...] = lax.fori_loop(0, 80, place_slot, jnp.full((8, 128), -1, jnp.int32))
    table_copy = pltpu.make_async_copy(tab, tabs, sem_loc.at[4])
    table_copy.start()

    cats = (cat_ref[...] - j * 4).astype(F32)
    cats = jnp.broadcast_to(jnp.concatenate([cats, cats], axis=1), (8, 128))
    catr[u] = cats
    col = jnp.transpose(cats)[0:64, 0:1]
    feats = x_ref[...].astype(F32)
    xg[z, yh * 2 + c] = x_ref[...]
    local[0].wait()
    total = jnp.zeros((64, 512), F32)
    for expert in range(4):
        masked = jnp.where(col == float(expert), feats, 0.0).astype(BF16)
        total = total + jnp.dot(masked, w[expert], preferred_element_type=F32)
    qg[z, yh * 2 + c] = total.astype(BF16)

    def hops(d, k):
        return 4 if (k == 0) == (d == R) else 3

    class Gather:
        def __init__(self, buf, sems):
            self.buf, self.sems = buf, sems

        def block(self, d, k, cc):
            return self.buf.at[(z + d + 8) % 8, (yh if k == 0 else 1 - yh) * 2 + cc]

        def pair(self, n):
            return self.sems.at[0, n], self.sems.at[1, n]

        def put(self, d, k, n, dev):
            block = self.block(d, k, c)
            send(block, block, *self.pair(n), dev)

        def begin(self):
            for d in (R, L):
                self.put(0, 0, (d * 2 + 0) * 4, at_z(DIR[d]))
            self.put(0, 0, 32, y_user)
            self.put(0, 0, 16, core)

        def cross(self):
            recv(self.block(0, 1, c), *self.pair(32), y_user)
            for d in (R, L):
                self.put(0, 1, (d * 2 + 1) * 4, at_z(DIR[d]))
            self.put(0, 1, 17, core)

        def step(self, s):
            for k in range(2):
                for d in (R, L):
                    if s > hops(d, k):
                        continue
                    off = -DIR[d] * s
                    n = (d * 2 + k) * 4 + s - 1
                    recv(self.block(off, k, c), *self.pair(n), at_z(-DIR[d]))
                    if s < hops(d, k):
                        self.put(off, k, n + 1, at_z(DIR[d]))
                    self.put(off, k, 16 + (off % 8) * 2 + k, core)

        def settle(self, d):
            for k in range(2):
                recv(self.block(d, k, 1 - c), *self.pair(16 + (d % 8) * 2 + k), core)

    queries = Gather(qg, sem_q)
    items = Gather(xg, sem_f)

    def build(d):
        zs = (z + d + 8) % 8

        def body(rb, _):
            for half in range(2):
                pos = rb * 16 + zs * 2 + half
                slot = tabs[pos // 128, pos % 128]
                scale = jnp.where(slot >= 0, 1.0 / 256, 0.0)
                tile = lvl[jnp.maximum(slot, 0)].astype(F32) * scale
                amat[zs, pl.ds(pl.multiple_of(rb * 128, 128), 128), half * 128 : half * 128 + 128] = tile.astype(BF16)
            return 0

        lax.fori_loop(0, 16, body, 0)

    def spread(offsets, first=False):
        for d in offsets:
            queries.settle(d)

        def body(r, _):
            part = None
            for d in offsets:
                zs = (z + d + 8) % 8
                term = jnp.dot(
                    amat[zs, pl.ds(pl.multiple_of(r * 256, 256), 256), :],
                    qg[zs].reshape(256, 512),
                    preferred_element_type=F32,
                )
                part = term if part is None else part + term
            part = part.reshape(2, 128, 512)
            acc[pl.ds(r * 2, 2)] = part if first else acc[pl.ds(r * 2, 2)] + part
            return 0

        lax.fori_loop(0, 8, body, 0)

    pl.semaphore_wait(barrier, 7)
    queries.begin()
    local[1].wait()
    table_copy.wait()
    build(0)
    queries.cross()
    build(1)
    build(-1)
    queries.step(1)
    spread((0,), True)
    build(2)
    queries.step(2)
    build(-2)
    spread((1, -1))
    build(3)
    queries.step(3)
    build(-3)
    build(4)
    spread((2, -2))
    queries.step(4)
    spread((3, -3))
    spread((4,))

    items.begin()

    def cats_start(k, _):
        remote(catr.at[u], catr.at[u], sem_cs.at[k], sem_cr.at[k], peer_u(k)).start()
        return 0

    def cats_wait(k, _):
        src = catr.at[(u + 32 - k) % 32]
        remote(src, src, sem_cs.at[k], sem_cr.at[k], peer_u(k)).wait()
        return 0

    low = lax.broadcasted_iota(jnp.int32, (8, 128), 1) < 64

    def cats_pair(p, _):
        catl[p] = jnp.where(low, catr[p * 2], catr[p * 2 + 1])
        return 0

    local[2].wait()
    local[3].wait()

    def ihops(d, h):
        return 2 if (h == 0) == (d == R) else 1

    def chunk(dx, y, h):
        return (y * 4 + (x + dx + 4) % 4) * 2 + h

    def ysel(k):
        return 1 - yl if k == 0 else yl

    def mx_send(d, k, h, s, value):
        mxs[d, k, h, s] = value.astype(BF16)
        send(mxs.at[d, k, h, s], mxr.at[d, k, h, s], sem_ixs.at[d, k, h, s], sem_ixr.at[d, k, h, s], at_x(DIR[d]))

    def mx_recv(d, k, h, s):
        recv(mxr.at[d, k, h, s], sem_ixs.at[d, k, h, s], sem_ixr.at[d, k, h, s], at_x(-DIR[d]))
        return mxr[d, k, h, s].astype(F32)

    combos = [(k, d, h) for k in range(2) for d in (R, L) for h in range(2)]
    for k, d, h in combos:
        if ihops(d, h) == 2:
            mx_send(d, k, h, 1, acc[chunk(2 * DIR[d], ysel(k), h)])
    for k, d, h in combos:
        if ihops(d, h) == 1:
            mx_send(d, k, h, 0, acc[chunk(DIR[d], ysel(k), h)])
    items.cross()
    lax.fori_loop(1, 32, cats_start, 0)
    for k, d, h in combos:
        if ihops(d, h) == 2:
            part = mx_recv(d, k, h, 1)
            mx_send(d, k, h, 0, acc[chunk(DIR[d], ysel(k), h)] + part)
    for h in range(2):
        value = acc[chunk(0, 1 - yl, h)] + mx_recv(R, 0, h, 0) + mx_recv(L, 0, h, 0)
        mys[h] = value.astype(BF16)
        send(mys.at[h], myr.at[h], sem_iys.at[h], sem_iyr.at[h], y_item)

    items.step(1)
    gain = gain_ref[...]
    gsum = jnp.zeros((1, 512), F32)
    for h in range(2):
        value = acc[chunk(0, yl, h)] + mx_recv(R, 1, h, 0) + mx_recv(L, 1, h, 0)
        recv(myr.at[h], sem_iys.at[h], sem_iyr.at[h], y_item)
        pre = uf[h * 128 : h * 128 + 128, :].astype(F32) + value + myr[h].astype(F32)
        grad = ct[h * 128 : h * 128 + 128, :].astype(F32)
        scaled = gain * grad
        inv = lax.rsqrt(jnp.sum(pre * pre, axis=-1, keepdims=True) * (1.0 / 512) + 1e-05)
        cross = jnp.sum(scaled * pre, axis=-1, keepdims=True) * (1.0 / 512)
        ugall[j, h] = (inv * scaled - inv * inv * inv * pre * cross).astype(BF16)
        gsum = gsum + jnp.sum(grad * pre * inv, axis=0, keepdims=True)
        mine = ugall.at[j, h]
        send(mine, mine, sem_gys.at[h], sem_gyr.at[h], y_item)
        for d in (R, L):
            send(mine, mine, sem_gxs.at[d, 0, h, 0], sem_gxr.at[d, 0, h, 0], at_x(DIR[d]))
    gs[...] = jnp.zeros((8, 128), F32)
    for t in range(4):
        gs[t : t + 1, :] = gsum[:, t * 128 : t * 128 + 128]

    def gain_i(k, _):
        remote(gs, gr.at[k], sem_g1s.at[k], sem_g1r.at[k], peer_i(k)).start()
        return 0

    lax.fori_loop(1, 8, gain_i, 0)

    def back(jj, first):
        ugt[...] = jnp.transpose(ugall[jj].reshape(256, 512).astype(F32)).astype(BF16)

        def body(zs, _):
            part = jnp.dot(
                ugt[...],
                amat[zs, pl.ds(pl.multiple_of(jj * 256, 256), 256), :],
                preferred_element_type=F32,
            )
            acc2[zs] = part if first else acc2[zs] + part
            return 0

        lax.fori_loop(0, 8, body, 0)
        ug_out[:, pl.ds(pl.multiple_of(jj * 256, 256), 256)] = ugt[pl.ds(pl.multiple_of(j * 64, 64), 64), :]

    def jat(dx, y):
        return y * 4 + (x + dx + 4) % 4

    def g_step(k, s):
        y = yl if k == 0 else 1 - yl
        for h in range(2):
            for d in (R, L):
                if s > ihops(d, h):
                    continue
                block = ugall.at[jat(-DIR[d] * s, y), h]
                recv(block, sem_gxs.at[d, k, h, s - 1], sem_gxr.at[d, k, h, s - 1], at_x(-DIR[d]))
                if s < ihops(d, h):
                    send(block, block, sem_gxs.at[d, k, h, s], sem_gxr.at[d, k, h, s], at_x(DIR[d]))

    for h in range(2):
        other = ugall.at[jat(0, 1 - yl), h]
        recv(other, sem_gys.at[h], sem_gyr.at[h], y_item)
        for d in (R, L):
            send(other, other, sem_gxs.at[d, 1, h, 0], sem_gxr.at[d, 1, h, 0], at_x(DIR[d]))
    items.step(2)
    back(j, True)
    g_step(0, 1)
    back(jat(0, 1 - yl), False)
    back(jat(1, yl), False)
    items.step(3)
    g_step(1, 1)
    back(jat(-1, yl), False)
    back(jat(1, 1 - yl), False)
    items.step(4)
    g_step(0, 2)
    lax.fori_loop(1, 32, cats_wait, 0)
    lax.fori_loop(0, 16, cats_pair, 0)
    for d in range(-3, 5):
        items.settle(d)
    back(jat(-1, 1 - yl), False)
    back(jat(2, yl), False)
    g_step(1, 2)
    back(jat(2, 1 - yl), False)

    def gain_i_wait(k, total):
        remote(gs, gr.at[k], sem_g1s.at[k], sem_g1r.at[k], peer_i(k)).wait()
        return total + gr[k]

    gt[...] = lax.fori_loop(1, 8, gain_i_wait, gs[...])

    def gain_u(k, _):
        remote(gt, gr2.at[k], sem_g2s.at[k], sem_g2r.at[k], peer_u(k)).start()
        return 0

    def urows(zs, y, cc):
        return pl.ds(pl.multiple_of((zs * 4 + y * 2 + cc) * 16, 16), 16)

    order = (4, 3, -3, 2, -2, 1, -1, 0)
    for d in order:
        zs = (z + d + 8) % 8
        for y in range(2):
            cs[zs, y] = acc2[:, urows(zs, y, 1 - c), :].astype(BF16)
        send(cs.at[zs], cr.at[zs], sem_ucs.at[d % 8], sem_ucr.at[d % 8], core)
    lax.fori_loop(1, 32, gain_u, 0)

    def core_recv(d):
        zs = (z + d + 8) % 8
        recv(cr.at[zs], sem_ucs.at[d % 8], sem_ucr.at[d % 8], core)

    def own_sum(d, y):
        zs = (z + d + 8) % 8
        return acc2[:, urows(zs, y, c), :] + cr[zs, y].astype(F32)

    def z_send(d, k, s, value):
        rs[d, k, s] = value.astype(BF16)
        send(rs.at[d, k, s], rr.at[d, k, s], sem_uzs.at[d, k, s], sem_uzr.at[d, k, s], at_z(DIR[d]))

    def z_recv(d, k, s):
        recv(rr.at[d, k, s], sem_uzs.at[d, k, s], sem_uzr.at[d, k, s], at_z(-DIR[d]))
        return rr[d, k, s].astype(F32)

    def uy(k):
        return 1 - yh if k == 0 else yh

    ucombos = [(k, d) for k in range(2) for d in (R, L)]
    for s in (4, 3, 2, 1):
        if s == 4:
            core_recv(4)
        else:
            core_recv(s)
            core_recv(-s)
        for k, d in ucombos:
            if hops(d, k) == s:
                z_send(d, k, s - 1, own_sum(DIR[d] * s, uy(k)))
        for k, d in ucombos:
            if hops(d, k) > s:
                z_send(d, k, s - 1, own_sum(DIR[d] * s, uy(k)) + z_recv(d, k, s))
    core_recv(0)
    ys[...] = (own_sum(0, 1 - yh) + z_recv(R, 0, 0) + z_recv(L, 0, 0)).astype(BF16)
    send(ys, yr, sem_uys.at[0], sem_uyr.at[0], y_user)
    mine = own_sum(0, yh) + z_recv(R, 1, 0) + z_recv(L, 1, 0)
    recv(yr, sem_uys.at[0], sem_uyr.at[0], y_user)
    mine = (mine + yr[...].astype(F32)).astype(BF16)
    for zs in range(8):
        for half in range(2):
            sumb[zs * 2 + half] = mine[zs, :, half * 128 : half * 128 + 128]

    st[u] = sumb[u // 2]

    def sums_start(k, _):
        remote(sumb.at[((u + k) % 32) // 2], st.at[u], sem_1s.at[k], sem_1r.at[k], peer_u(k)).start()
        return 0

    lax.fori_loop(1, 32, sums_start, 0)

    for p in range(16):
        cat16 = jnp.concatenate([catl[p], catl[p]], axis=0)
        value = sumb[p].astype(F32)
        for expert in range(4):
            ms[expert * 16 : expert * 16 + 16, p * 128 : p * 128 + 128] = jnp.where(
                cat16 == float(expert), value, 0.0
            ).astype(BF16)
    grads = jnp.zeros((64, 512), F32)
    for zs in range(8):
        grads = grads + jnp.dot(
            ms[:, zs * 256 : zs * 256 + 256], xg[zs].reshape(256, 512), preferred_element_type=F32
        )
    wide = jnp.transpose(jnp.concatenate([grads, grads], axis=0)).reshape(32, 2, 8, 128)
    es[...] = jnp.where(low[None], wide[:, 0], wide[:, 1])
    er[u] = es[u]

    def grads_start(k, _):
        remote(es.at[(u + k) % 32], er.at[u], sem_2s.at[k], sem_2r.at[k], peer_u(k)).start()
        return 0

    lax.fori_loop(1, 32, grads_start, 0)

    def gain_u_wait(k, total):
        remote(gt, gr2.at[k], sem_g2s.at[k], sem_g2r.at[k], peer_u(k)).wait()
        return total + gr2[k]

    gs2 = lax.fori_loop(1, 32, gain_u_wait, gt[...])
    gr[0] = gs2
    grow = gr[0, pl.ds(j // 2, 1), :]
    gg_out[...] = jnp.where(j % 2 == 0, grow[:, 0:64], grow[:, 64:128])

    def sums_wait(k, _):
        dst = st.at[(u + 32 - k) % 32]
        remote(dst, dst, sem_1s.at[k], sem_1r.at[k], peer_u(k)).wait()
        return 0

    lax.fori_loop(1, 32, sums_wait, 0)
    sums = st[...].reshape(512, 128).astype(F32)
    cat1 = catl[u // 2][0:1, :]
    total = jnp.zeros((512, 128), F32)
    for expert in range(4):
        masked = jnp.where(cat1 == float(expert), sums, 0.0).astype(BF16)
        total = total + jnp.dot(w[expert], masked, preferred_element_type=F32)
    igt[...] = jnp.transpose(total)
    ig_out[...] = igt[pl.ds(pl.multiple_of(c * 64, 64), 64), :].astype(BF16)

    def grads_wait(k, _):
        dst = er.at[(u + 32 - k) % 32]
        remote(dst, dst, sem_2s.at[k], sem_2r.at[k], peer_u(k)).wait()
        return 0

    lax.fori_loop(1, 32, grads_wait, 0)
    lane = lax.broadcasted_iota(jnp.int32, (8, 128), 1) // 16
    for expert in range(4):
        for half in range(2):
            for t in range(4):
                line = jnp.zeros((8, 128), F32)
                for k in range(8):
                    moved = pltpu.roll(er[t * 8 + k], (k * 16 - half * 64 - expert * 16) % 128, 1)
                    line = jnp.where(lane == k, moved, line)
                eg_out[expert, half * 8 : half * 8 + 8, t * 128 : t * 128 + 128] = line

    for copy in sent:
        copy.wait_send()


def settle(ug, ig, eg, gg, ug_out, ig_out, eg_out, gg_out, sems):
    copies = [
        pltpu.make_async_copy(src, dst, sems.at[n])
        for n, (src, dst) in enumerate(((ug, ug_out), (ig, ig_out), (eg, eg_out), (gg, gg_out)))
    ]
    for copy in copies:
        copy.start()
    for copy in copies:
        copy.wait()


def on_device(
    user_feat, cotangent, gain, item_feat, categories, expert_w, tile_place, tile_level, tile_count
):
    vmem = pl.BlockSpec(memory_space=pltpu.VMEM)
    smem = pl.BlockSpec(memory_space=pltpu.SMEM)
    hbm = pl.BlockSpec(memory_space=pl.ANY)
    V = pltpu.VMEM
    scratch = [
        V((8, 4, 64, 512), BF16), V((8, 4, 64, 512), BF16), V((4, 512, 512), BF16), V((80, 128, 128), jnp.int32),
        V((8, 2048, 256), BF16), V((16, 128, 512), F32),
        V((256, 512), BF16), V((256, 512), BF16), V((32, 8, 128), F32), V((16, 8, 128), F32),
        V((8, 128), jnp.int32), pltpu.SMEM((8, 128), jnp.int32),
        V((2, 2, 2, 2, 128, 512), BF16), V((2, 2, 2, 2, 128, 512), BF16),
        V((2, 128, 512), BF16), V((2, 128, 512), BF16),
        V((8, 2, 128, 512), BF16), V((512, 256), BF16), V((8, 512, 256), F32),
        V((8, 2, 8, 16, 256), BF16), V((8, 2, 8, 16, 256), BF16),
        V((2, 2, 4, 8, 16, 256), BF16), V((2, 2, 4, 8, 16, 256), BF16),
        V((8, 16, 256), BF16), V((8, 16, 256), BF16),
        V((16, 16, 128), BF16), V((32, 16, 128), BF16), V((64, 2048), BF16),
        V((32, 8, 128), F32), V((32, 8, 128), F32), V((128, 512), F32),
        V((8, 128), F32), V((8, 8, 128), F32), V((8, 128), F32), V((32, 8, 128), F32),
        DMA((5,)), DMA((32,)), DMA((32,)), DMA((2, 33)), DMA((2, 33)),
        DMA((2, 2, 2, 2)), DMA((2, 2, 2, 2)), DMA((2,)), DMA((2,)),
        DMA((2, 2, 2, 2)), DMA((2, 2, 2, 2)), DMA((2,)), DMA((2,)),
        DMA((8,)), DMA((8,)), DMA((2, 2, 4)), DMA((2, 2, 4)), DMA((1,)), DMA((1,)),
        DMA((32,)), DMA((32,)), DMA((32,)), DMA((32,)), DMA((8,)), DMA((8,)), DMA((32,)), DMA((32,)),
    ]
    shapes = (
        jax.ShapeDtypeStruct((64, 2048), BF16),
        jax.ShapeDtypeStruct((64, 512), BF16),
        jax.ShapeDtypeStruct((4, 16, 512), F32),
        jax.ShapeDtypeStruct((1, 64), F32),
    )
    parts = pl.pallas_call(
        layer,
        out_shape=shapes,
        in_specs=[vmem, vmem, vmem, smem, smem, hbm, hbm, hbm, hbm],
        out_specs=(vmem, vmem, vmem, vmem),
        scratch_shapes=scratch,
        compiler_params=pltpu.CompilerParams(
            collective_id=0, has_side_effects=True, vmem_limit_bytes=60 * 2**20
        ),
    )(
        item_feat[0], categories, gain[None, :], tile_place[0, 0], tile_count, expert_w, tile_level[0, 0],
        user_feat, cotangent,
    )
    ug, ig, eg, gg = pl.pallas_call(
        settle,
        out_shape=shapes,
        in_specs=[hbm] * 4,
        out_specs=(hbm,) * 4,
        scratch_shapes=[DMA((4,))],
    )(*parts)
    return ug.T, ig[None], eg, gg[0]


def solution(mesh):
    placed = (
        P("user", None),
        P("user", None),
        P(),
        P("item", "user", None),
        P("item", "user"),
        P("item", None, None),
        P("user", "item", None),
        P("user", "item", None, None, None),
        P("user", "item"),
    )
    return jax.shard_map(
        on_device,
        mesh=mesh,
        in_specs=placed,
        out_specs=(P("user", "item"), P("item", "user", None), P("item", "user", None), P("item")),
        check_vma=False,
    )
```

```python
import jax
import jax.numpy as jnp
from jax import lax
from jax.experimental import pallas as pl
from jax.experimental.pallas import tpu as pltpu
from jax.sharding import PartitionSpec as P

MESH = pl.DeviceIdType.MESH
F32 = jnp.float32
BF16 = jnp.bfloat16
DMA = pltpu.SemaphoreType.DMA
R, L = 0, 1
DIR = (1, -1)


def layer(
    x_ref, cat_ref, gain_ref, place_ref, count_ref, w_hbm, lvl_hbm, uf_hbm, ct_hbm,
    ug_out, ig_out, eg_out, gg_out,
    xg, qg, w, lvl, amat, acc, uf, ct, catr, catl, tab, tabs,
    mxs, mxr, mys, myr, ugall, ugt, acc2,
    cs, cr, rs, rr, ys, yr, sumb, st, ms, es, er, igt, gs, gr, gt, gr2,
    sem_loc, sem_cs, sem_cr, sem_q, sem_f,
    sem_ixs, sem_ixr, sem_iys, sem_iyr, sem_gxs, sem_gxr, sem_gys, sem_gyr,
    sem_ucs, sem_ucr, sem_uzs, sem_uzr, sem_uys, sem_uyr,
    sem_1s, sem_1r, sem_2s, sem_2r, sem_g1s, sem_g1r, sem_g2s, sem_g2r,
):
    u = lax.axis_index("user")
    j = lax.axis_index("item")
    z, yh, c = u // 4, (u // 2) % 2, u % 2
    yl, x = j // 4, j % 4

    def at_z(d):
        return (((z + d + 8) % 8) * 4 + yh * 2 + c, j)

    def at_x(d):
        return (u, yl * 4 + (x + d + 4) % 4)

    y_user = (z * 4 + (1 - yh) * 2 + c, j)
    core = (z * 4 + yh * 2 + 1 - c, j)
    y_item = (u, (1 - yl) * 4 + x)

    def peer_u(k):
        return ((u + k) % 32, j)

    def peer_i(k):
        return (u, ((yl + k // 4) % 2) * 4 + (x + k % 4) % 4)

    sent = []

    def remote(src, dst, ssem, rsem, dev):
        return pltpu.make_async_remote_copy(
            src_ref=src, dst_ref=dst, send_sem=ssem, recv_sem=rsem, device_id=dev, device_id_type=MESH
        )

    def send(src, dst, ssem, rsem, dev):
        copy = remote(src, dst, ssem, rsem, dev)
        copy.start()
        sent.append(copy)

    def recv(dst, ssem, rsem, dev):
        remote(dst, dst, ssem, rsem, dev).wait_recv()

    barrier = pltpu.get_barrier_semaphore()
    for dev in (at_z(1), at_z(-1), at_x(1), at_x(-1), y_user, y_item, core):
        pl.semaphore_signal(barrier, inc=1, device_id=dev, device_id_type=MESH)

    rows = pl.ds(pl.multiple_of(j * 256, 256), 256)
    local = [
        pltpu.make_async_copy(w_hbm, w, sem_loc.at[1]),
        pltpu.make_async_copy(lvl_hbm, lvl, sem_loc.at[0]),
        pltpu.make_async_copy(uf_hbm.at[rows], uf, sem_loc.at[2]),
        pltpu.make_async_copy(ct_hbm.at[rows], ct, sem_loc.at[3]),
    ]
    for copy in local:
        copy.start()

    spot = lax.broadcasted_iota(jnp.int32, (8, 128), 0) * 128 + lax.broadcasted_iota(jnp.int32, (8, 128), 1)

    def place_slot(s, table):
        key = jnp.where(s < count_ref[0, 0], place_ref[s], -1)
        return jnp.where(spot == key, s, table)

    tab[...] = lax.fori_loop(0, 80, place_slot, jnp.full((8, 128), -1, jnp.int32))
    table_copy = pltpu.make_async_copy(tab, tabs, sem_loc.at[4])
    table_copy.start()

    cats = (cat_ref[...] - j * 4).astype(F32)
    cats = jnp.broadcast_to(jnp.concatenate([cats, cats], axis=1), (8, 128))
    catr[u] = cats
    col = jnp.transpose(cats)[0:64, 0:1]
    feats = x_ref[...].astype(F32)
    xg[z, yh * 2 + c] = x_ref[...]
    local[0].wait()
    total = jnp.zeros((64, 512), F32)
    for expert in range(4):
        masked = jnp.where(col == float(expert), feats, 0.0).astype(BF16)
        total = total + jnp.dot(masked, w[expert], preferred_element_type=F32)
    for fh in range(2):
        qg[fh, z, yh * 2 + c] = total[:, fh * 256 : fh * 256 + 256].astype(BF16)

    def hops(d, k):
        return 4 if (k == 0) == (d == R) else 3

    class Gather:
        def __init__(self, buf, sems):
            self.buf, self.sems = buf, sems

        def block(self, d, k, cc):
            return self.buf.at[(z + d + 8) % 8, (yh if k == 0 else 1 - yh) * 2 + cc]

        def pair(self, n):
            return self.sems.at[0, n], self.sems.at[1, n]

        def put(self, d, k, n, dev):
            block = self.block(d, k, c)
            send(block, block, *self.pair(n), dev)

        def begin(self):
            for d in (R, L):
                self.put(0, 0, (d * 2 + 0) * 4, at_z(DIR[d]))
            self.put(0, 0, 32, y_user)
            self.put(0, 0, 16, core)

        def cross(self):
            recv(self.block(0, 1, c), *self.pair(32), y_user)
            for d in (R, L):
                self.put(0, 1, (d * 2 + 1) * 4, at_z(DIR[d]))
            self.put(0, 1, 17, core)

        def step(self, s):
            for k in range(2):
                for d in (R, L):
                    if s > hops(d, k):
                        continue
                    off = -DIR[d] * s
                    n = (d * 2 + k) * 4 + s - 1
                    recv(self.block(off, k, c), *self.pair(n), at_z(-DIR[d]))
                    if s < hops(d, k):
                        self.put(off, k, n + 1, at_z(DIR[d]))
                    self.put(off, k, 16 + (off % 8) * 2 + k, core)

        def settle(self, d):
            for k in range(2):
                recv(self.block(d, k, 1 - c), *self.pair(16 + (d % 8) * 2 + k), core)

    queries = [Gather(qg.at[fh], sem_q.at[fh]) for fh in range(2)]
    items = Gather(xg, sem_f)

    def build(zs):
        def body(rb, _):
            for half in range(2):
                pos = rb * 16 + zs * 2 + half
                slot = tabs[pos // 128, pos % 128]
                scale = jnp.where(slot >= 0, 1.0 / 256, 0.0)
                tile = lvl[jnp.maximum(slot, 0)].astype(F32) * scale
                col0 = zs * 256 + half * 128
                amat[pl.ds(pl.multiple_of(rb * 128, 128), 128), col0 : col0 + 128] = tile.astype(BF16)
            return 0

        lax.fori_loop(0, 16, body, 0)

    def ihops(d, h):
        return 2 if (h == 0) == (d == R) else 1

    def jat(dx, y):
        return y * 4 + (x + dx + 4) % 4

    def ysel(k):
        return 1 - yl if k == 0 else yl

    def product(fh, dx):
        for k in range(2):
            jt = jat(dx, ysel(k))
            part = jnp.dot(
                amat[pl.ds(pl.multiple_of(jt * 256, 256), 256), :],
                qg[fh].reshape(2048, 256),
                preferred_element_type=F32,
            )
            acc[fh, pl.ds(jt * 2, 2)] = part.reshape(2, 128, 256)

    def term(fh, dx, k, h):
        return acc[fh, jat(dx, ysel(k)) * 2 + h]

    def mx_send(fh, d, k, h, s, value):
        n = (fh, d, k, h, s)
        mxs[n] = value.astype(BF16)
        send(mxs.at[n], mxr.at[n], sem_ixs.at[n], sem_ixr.at[n], at_x(DIR[d]))

    def mx_recv(fh, d, k, h, s):
        n = (fh, d, k, h, s)
        recv(mxr.at[n], sem_ixs.at[n], sem_ixr.at[n], at_x(-DIR[d]))
        return mxr[n].astype(F32)

    combos = [(k, d, h) for k in range(2) for d in (R, L) for h in range(2)]

    def far(fh):
        product(fh, 2)
        for k, d, h in combos:
            if ihops(d, h) == 2:
                mx_send(fh, d, k, h, 1, term(fh, 2, k, h))

    def near(fh):
        product(fh, 1)
        product(fh, -1)
        for k, d, h in combos:
            if ihops(d, h) == 1:
                mx_send(fh, d, k, h, 0, term(fh, DIR[d], k, h))

    def relay(fh, want):
        for k, d, h in combos:
            if k == want and ihops(d, h) == 2:
                mx_send(fh, d, k, h, 0, term(fh, DIR[d], k, h) + mx_recv(fh, d, k, h, 1))

    def pair_send(fh):
        for h in range(2):
            value = term(fh, 0, 0, h) + mx_recv(fh, R, 0, h, 0) + mx_recv(fh, L, 0, h, 0)
            mys[fh, h] = value.astype(BF16)
            send(mys.at[fh, h], myr.at[fh, h], sem_iys.at[fh, h], sem_iyr.at[fh, h], y_item)

    def summed(fh, h):
        value = term(fh, 0, 1, h) + mx_recv(fh, R, 1, h, 0) + mx_recv(fh, L, 1, h, 0)
        recv(myr.at[fh, h], sem_iys.at[fh, h], sem_iyr.at[fh, h], y_item)
        return value + myr[fh, h].astype(F32)

    def cats_start(k, _):
        remote(catr.at[u], catr.at[u], sem_cs.at[k], sem_cr.at[k], peer_u(k)).start()
        return 0

    def cats_wait(k, _):
        src = catr.at[(u + 32 - k) % 32]
        remote(src, src, sem_cs.at[k], sem_cr.at[k], peer_u(k)).wait()
        return 0

    low = lax.broadcasted_iota(jnp.int32, (8, 128), 1) < 64

    def cats_pair(p, _):
        catl[p] = jnp.where(low, catr[p * 2], catr[p * 2 + 1])
        return 0

    def all_here(fh):
        for d in range(-3, 5):
            queries[fh].settle(d)

    pl.semaphore_wait(barrier, 7)
    queries[0].begin()
    local[1].wait()
    table_copy.wait()
    build(0)
    queries[0].cross()
    queries[1].begin()
    build(1)
    build(2)
    queries[0].step(1)
    queries[1].cross()
    build(3)
    build(4)
    queries[0].step(2)
    queries[1].step(1)
    build(5)
    build(6)
    queries[0].step(3)
    queries[1].step(2)
    build(7)
    queries[0].step(4)
    all_here(0)
    far(0)
    queries[1].step(3)
    near(0)
    queries[1].step(4)
    product(0, 0)
    relay(0, 0)
    relay(0, 1)
    all_here(1)
    far(1)
    items.begin()
    near(1)
    pair_send(0)
    product(1, 0)
    items.cross()
    relay(1, 0)
    relay(1, 1)
    lax.fori_loop(1, 32, cats_start, 0)
    pair_send(1)
    items.step(1)

    local[2].wait()
    local[3].wait()
    gain = [gain_ref[:, fh * 256 : fh * 256 + 256] for fh in range(2)]
    gsum = [jnp.zeros((1, 256), F32) for fh in range(2)]

    def g_put(fh, h, k, n, dev):
        block = ugall.at[fh, jat(0, yl if k == 0 else 1 - yl), h]
        send(block, block, *n, dev)

    def g_cross_start(fh, h):
        g_put(fh, h, 0, (sem_gys.at[fh, h], sem_gyr.at[fh, h]), y_item)

    def g_ring_start(fh, h, k):
        for d in (R, L):
            g_put(fh, h, k, (sem_gxs.at[fh, d, k, h, 0], sem_gxr.at[fh, d, k, h, 0]), at_x(DIR[d]))

    def g_cross(fh):
        for h in range(2):
            recv(ugall.at[fh, jat(0, 1 - yl), h], sem_gys.at[fh, h], sem_gyr.at[fh, h], y_item)
            g_ring_start(fh, h, 1)

    def g_step(fh, k, s):
        y = yl if k == 0 else 1 - yl
        for h in range(2):
            for d in (R, L):
                if s > ihops(d, h):
                    continue
                block = ugall.at[fh, jat(-DIR[d] * s, y), h]
                n = (fh, d, k, h, s - 1)
                recv(block, sem_gxs.at[n], sem_gxr.at[n], at_x(-DIR[d]))
                if s < ihops(d, h):
                    n = (fh, d, k, h, s)
                    send(block, block, sem_gxs.at[n], sem_gxr.at[n], at_x(DIR[d]))

    for h in range(2):
        feat_rows = slice(h * 128, h * 128 + 128)
        pre, grad = [], []
        for fh in range(2):
            cols = slice(fh * 256, fh * 256 + 256)
            pre.append(uf[feat_rows, cols].astype(F32) + summed(fh, h))
            grad.append(ct[feat_rows, cols].astype(F32))
        squares = sum(jnp.sum(p * p, axis=-1, keepdims=True) for p in pre)
        crossed = sum(jnp.sum(gain[fh] * grad[fh] * pre[fh], axis=-1, keepdims=True) for fh in range(2))
        inv = lax.rsqrt(squares * (1.0 / 512) + 1e-05)
        factor = inv * inv * inv * (crossed * (1.0 / 512))
        for fh in range(2):
            ugall[fh, j, h] = (inv * (gain[fh] * grad[fh]) - factor * pre[fh]).astype(BF16)
            gsum[fh] = gsum[fh] + jnp.sum(grad[fh] * pre[fh] * inv, axis=0, keepdims=True)
        g_cross_start(0, h)
        g_ring_start(0, h, 0)
    for h in range(2):
        g_cross_start(1, h)
    gs[...] = jnp.zeros((8, 128), F32)
    for t in range(4):
        gs[t : t + 1, :] = gsum[t // 2][:, (t % 2) * 128 : (t % 2) * 128 + 128]

    def gain_i(k, _):
        remote(gs, gr.at[k], sem_g1s.at[k], sem_g1r.at[k], peer_i(k)).start()
        return 0

    lax.fori_loop(1, 8, gain_i, 0)

    def back(fh, dx, y, first=False):
        jj = jat(dx, y)
        ugt[...] = jnp.transpose(ugall[fh, jj].reshape(256, 256).astype(F32)).astype(BF16)
        for zs in range(8):
            part = jnp.dot(
                ugt[...],
                amat[pl.ds(pl.multiple_of(jj * 256, 256), 256), zs * 256 : zs * 256 + 256],
                preferred_element_type=F32,
            )
            acc2[fh, zs] = part if first else acc2[fh, zs] + part

        @pl.when(j // 4 == fh)
        def _():
            ug_out[:, pl.ds(pl.multiple_of(jj * 256, 256), 256)] = ugt[
                pl.ds(pl.multiple_of((j % 4) * 64, 64), 64), :
            ]

    def piece(fh, zs, y, cc):
        v = acc2[fh, :, pl.ds(pl.multiple_of((zs * 4 + y * 2 + cc) * 8, 8), 8), :]
        return jnp.concatenate([v[0:4], v[4:8]], axis=1)

    def core_start(fh):
        for d in (4, 3, -3, 2, -2, 1, -1, 0):
            zs = (z + d + 8) % 8
            for y in range(2):
                cs[fh, zs, y] = piece(fh, zs, y, 1 - c).astype(BF16)
            send(cs.at[fh, zs], cr.at[fh, zs], sem_ucs.at[fh, d % 8], sem_ucr.at[fh, d % 8], core)

    def core_recv(fh, d):
        recv(cr.at[fh, (z + d + 8) % 8], sem_ucs.at[fh, d % 8], sem_ucr.at[fh, d % 8], core)

    def own_sum(fh, d, y):
        zs = (z + d + 8) % 8
        return piece(fh, zs, y, c) + cr[fh, zs, y].astype(F32)

    def z_send(fh, d, k, s, value):
        n = (fh, d, k, s)
        rs[n] = value.astype(BF16)
        send(rs.at[n], rr.at[n], sem_uzs.at[n], sem_uzr.at[n], at_z(DIR[d]))

    def z_recv(fh, d, k, s):
        n = (fh, d, k, s)
        recv(rr.at[n], sem_uzs.at[n], sem_uzr.at[n], at_z(-DIR[d]))
        return rr[n].astype(F32)

    def uy(k):
        return 1 - yh if k == 0 else yh

    ucombos = [(k, d) for k in range(2) for d in (R, L)]

    def ring(fh, s):
        core_recv(fh, s)
        if s < 4:
            core_recv(fh, -s)
        for k, d in ucombos:
            if hops(d, k) == s:
                z_send(fh, d, k, s - 1, own_sum(fh, DIR[d] * s, uy(k)))
        for k, d in ucombos:
            if hops(d, k) > s:
                z_send(fh, d, k, s - 1, own_sum(fh, DIR[d] * s, uy(k)) + z_recv(fh, d, k, s))

    def u_cross(fh):
        core_recv(fh, 0)
        ys[fh] = (own_sum(fh, 0, 1 - yh) + z_recv(fh, R, 0, 0) + z_recv(fh, L, 0, 0)).astype(BF16)
        send(ys.at[fh], yr.at[fh], sem_uys.at[fh], sem_uyr.at[fh], y_user)

    def u_final(fh):
        mine = own_sum(fh, 0, yh) + z_recv(fh, R, 1, 0) + z_recv(fh, L, 1, 0)
        recv(yr.at[fh], sem_uys.at[fh], sem_uyr.at[fh], y_user)
        return mine + yr[fh].astype(F32)

    items.step(2)
    back(0, 0, yl, True)
    g_cross(0)
    g_step(0, 0, 1)
    for h in range(2):
        g_ring_start(1, h, 0)
    back(0, 1, yl)
    back(0, -1, yl)
    g_step(0, 1, 1)
    items.step(3)
    g_cross(1)
    back(0, 0, 1 - yl)
    back(0, 1, 1 - yl)
    back(0, -1, 1 - yl)
    g_step(0, 0, 2)
    back(0, 2, yl)
    items.step(4)
    g_step(0, 1, 2)
    back(0, 2, 1 - yl)
    core_start(0)
    g_step(1, 0, 1)
    back(1, 0, yl, True)
    ring(0, 4)
    ring(0, 3)
    back(1, 0, 1 - yl)
    g_step(1, 1, 1)
    ring(0, 2)
    back(1, 1, yl)
    back(1, -1, yl)
    g_step(1, 0, 2)
    ring(0, 1)
    back(1, 1, 1 - yl)
    back(1, -1, 1 - yl)
    back(1, 2, yl)
    u_cross(0)
    g_step(1, 1, 2)
    back(1, 2, 1 - yl)
    core_start(1)
    lax.fori_loop(1, 32, cats_wait, 0)
    lax.fori_loop(0, 16, cats_pair, 0)
    for d in range(-3, 5):
        items.settle(d)

    def gain_i_wait(k, total):
        remote(gs, gr.at[k], sem_g1s.at[k], sem_g1r.at[k], peer_i(k)).wait()
        return total + gr[k]

    gt[...] = lax.fori_loop(1, 8, gain_i_wait, gs[...])

    def gain_u(k, _):
        remote(gt, gr2.at[k], sem_g2s.at[k], sem_g2r.at[k], peer_u(k)).start()
        return 0

    ring(1, 4)
    ring(1, 3)
    lax.fori_loop(1, 32, gain_u, 0)
    ring(1, 2)
    ring(1, 1)
    u_cross(1)
    mine = jnp.concatenate(
        [
            jnp.concatenate([value[:, 0:8], value[:, 8:16]], axis=0)
            for value in (u_final(0), u_final(1))
        ],
        axis=1,
    ).astype(BF16)
    for zs in range(8):
        for half in range(2):
            sumb[zs * 2 + half] = mine[zs, :, half * 128 : half * 128 + 128]

    st[u] = sumb[u // 2]

    def sums_start(k, _):
        remote(sumb.at[((u + k) % 32) // 2], st.at[u], sem_1s.at[k], sem_1r.at[k], peer_u(k)).start()
        return 0

    lax.fori_loop(1, 32, sums_start, 0)

    for p in range(16):
        cat16 = jnp.concatenate([catl[p], catl[p]], axis=0)
        value = sumb[p].astype(F32)
        for expert in range(4):
            ms[expert * 16 : expert * 16 + 16, p * 128 : p * 128 + 128] = jnp.where(
                cat16 == float(expert), value, 0.0
            ).astype(BF16)
    grads = jnp.zeros((64, 512), F32)
    for zs in range(8):
        grads = grads + jnp.dot(
            ms[:, zs * 256 : zs * 256 + 256], xg[zs].reshape(256, 512), preferred_element_type=F32
        )
    wide = jnp.transpose(jnp.concatenate([grads, grads], axis=0)).reshape(32, 2, 8, 128)
    es[...] = jnp.where(low[None], wide[:, 0], wide[:, 1])
    er[u] = es[u]

    def grads_start(k, _):
        remote(es.at[(u + k) % 32], er.at[u], sem_2s.at[k], sem_2r.at[k], peer_u(k)).start()
        return 0

    lax.fori_loop(1, 32, grads_start, 0)

    def gain_u_wait(k, total):
        remote(gt, gr2.at[k], sem_g2s.at[k], sem_g2r.at[k], peer_u(k)).wait()
        return total + gr2[k]

    gs2 = lax.fori_loop(1, 32, gain_u_wait, gt[...])
    gr[0] = gs2
    grow = gr[0, pl.ds(j // 2, 1), :]
    gg_out[...] = jnp.where(j % 2 == 0, grow[:, 0:64], grow[:, 64:128])

    def sums_wait(k, _):
        dst = st.at[(u + 32 - k) % 32]
        remote(dst, dst, sem_1s.at[k], sem_1r.at[k], peer_u(k)).wait()
        return 0

    lax.fori_loop(1, 32, sums_wait, 0)
    wide = st[...].astype(F32)
    sums = jnp.concatenate([wide[:, 0:8], wide[:, 8:16]], axis=0).reshape(512, 128)
    cat1 = catl[u // 2][0:1, :]
    total = jnp.zeros((512, 128), F32)
    for expert in range(4):
        masked = jnp.where(cat1 == float(expert), sums, 0.0).astype(BF16)
        total = total + jnp.dot(w[expert], masked, preferred_element_type=F32)
    igt[...] = jnp.transpose(total)
    ig_out[...] = igt[pl.ds(pl.multiple_of(c * 64, 64), 64), :].astype(BF16)

    def grads_wait(k, _):
        dst = er.at[(u + 32 - k) % 32]
        remote(dst, dst, sem_2s.at[k], sem_2r.at[k], peer_u(k)).wait()
        return 0

    lax.fori_loop(1, 32, grads_wait, 0)
    lane = lax.broadcasted_iota(jnp.int32, (8, 128), 1) // 8
    for expert in range(4):
        for half in range(2):
            for t in range(4):
                line = jnp.zeros((8, 128), F32)
                for k in range(16):
                    shift = k * 8 - half * 64 - expert * 16 - (t // 2) * 8
                    moved = pltpu.roll(er[(t % 2) * 16 + k], shift % 128, 1)
                    line = jnp.where(lane == k, moved, line)
                eg_out[expert, half * 8 : half * 8 + 8, t * 128 : t * 128 + 128] = line

    for copy in sent:
        copy.wait_send()


def settle(ug, ig, eg, gg, ug_out, ig_out, eg_out, gg_out):
    for src, dst in ((ug, ug_out), (ig, ig_out), (eg, eg_out), (gg, gg_out)):
        dst[...] = src[...]


def on_device(
    user_feat, cotangent, gain, item_feat, categories, expert_w, tile_place, tile_level, tile_count
):
    vmem = pl.BlockSpec(memory_space=pltpu.VMEM)
    smem = pl.BlockSpec(memory_space=pltpu.SMEM)
    hbm = pl.BlockSpec(memory_space=pl.ANY)
    V = pltpu.VMEM
    scratch = [
        V((8, 4, 64, 512), BF16), V((2, 8, 4, 64, 256), BF16), V((4, 512, 512), BF16), V((80, 128, 128), jnp.int32),
        V((2048, 2048), BF16), V((2, 16, 128, 256), F32),
        V((256, 512), BF16), V((256, 512), BF16), V((32, 8, 128), F32), V((16, 8, 128), F32),
        V((8, 128), jnp.int32), pltpu.SMEM((8, 128), jnp.int32),
        V((2, 2, 2, 2, 2, 128, 256), BF16), V((2, 2, 2, 2, 2, 128, 256), BF16),
        V((2, 2, 128, 256), BF16), V((2, 2, 128, 256), BF16),
        V((2, 8, 2, 128, 256), BF16), V((256, 256), BF16), V((2, 8, 256, 256), F32),
        V((2, 8, 2, 4, 16, 256), BF16), V((2, 8, 2, 4, 16, 256), BF16),
        V((2, 2, 2, 4, 4, 16, 256), BF16), V((2, 2, 2, 4, 4, 16, 256), BF16),
        V((2, 4, 16, 256), BF16), V((2, 4, 16, 256), BF16),
        V((16, 16, 128), BF16), V((32, 16, 128), BF16), V((64, 2048), BF16),
        V((32, 8, 128), F32), V((32, 8, 128), F32), V((128, 512), F32),
        V((8, 128), F32), V((8, 8, 128), F32), V((8, 128), F32), V((32, 8, 128), F32),
        DMA((5,)), DMA((32,)), DMA((32,)), DMA((2, 2, 33)), DMA((2, 33)),
        DMA((2, 2, 2, 2, 2)), DMA((2, 2, 2, 2, 2)), DMA((2, 2)), DMA((2, 2)),
        DMA((2, 2, 2, 2, 2)), DMA((2, 2, 2, 2, 2)), DMA((2, 2)), DMA((2, 2)),
        DMA((2, 8)), DMA((2, 8)), DMA((2, 2, 2, 4)), DMA((2, 2, 2, 4)), DMA((2,)), DMA((2,)),
        DMA((32,)), DMA((32,)), DMA((32,)), DMA((32,)), DMA((8,)), DMA((8,)), DMA((32,)), DMA((32,)),
    ]
    shapes = (
        jax.ShapeDtypeStruct((64, 2048), BF16),
        jax.ShapeDtypeStruct((64, 512), BF16),
        jax.ShapeDtypeStruct((4, 16, 512), F32),
        jax.ShapeDtypeStruct((1, 64), F32),
    )
    parts = pl.pallas_call(
        layer,
        out_shape=shapes,
        in_specs=[vmem, vmem, vmem, smem, smem, hbm, hbm, hbm, hbm],
        out_specs=(vmem, vmem, vmem, vmem),
        scratch_shapes=scratch,
        compiler_params=pltpu.CompilerParams(
            collective_id=0, has_side_effects=True, vmem_limit_bytes=60 * 2**20
        ),
    )(
        item_feat[0], categories, gain[None, :], tile_place[0, 0], tile_count, expert_w, tile_level[0, 0],
        user_feat, cotangent,
    )
    ug, ig, eg, gg = pl.pallas_call(
        settle,
        out_shape=shapes,
        in_specs=[vmem] * 4,
        out_specs=(vmem,) * 4,
    )(*parts)
    return ug.T, ig[None], eg, gg[0]


def solution(mesh):
    placed = (
        P("user", None),
        P("user", None),
        P(),
        P("item", "user", None),
        P("item", "user"),
        P("item", None, None),
        P("user", "item", None),
        P("user", "item", None, None, None),
        P("user", "item"),
    )
    return jax.shard_map(
        on_device,
        mesh=mesh,
        in_specs=placed,
        out_specs=(P("user", "item"), P("item", "user", None), P("item", "user", None), P("item")),
        check_vma=False,
    )
```

```python
import jax
import jax.numpy as jnp
from jax import lax
from jax.experimental import pallas as pl
from jax.experimental.pallas import tpu as pltpu
from jax.sharding import PartitionSpec as P

MESH = pl.DeviceIdType.MESH
F32 = jnp.float32
BF16 = jnp.bfloat16
DMA = pltpu.SemaphoreType.DMA
R, L = 0, 1
DIR = (1, -1)


def layer(
    x_ref, cat_ref, gain_ref, place_ref, count_ref, w_hbm, lvl_hbm, uf_hbm, ct_hbm,
    ug_out, ig_out, eg_out, gg_out,
    xg, qg, w, lvl, amat, acc, uf, ct, catr, catl, tab, tabs,
    mxs, mxr, mys, myr, ugall, ugt, acc2,
    cs, cr, rs, rr, ys, yr, sumb, st, ms, es, er, igt, gs, gr, gt, gr2,
    sem_loc, sem_cs, sem_cr, sem_q, sem_f,
    sem_ixs, sem_ixr, sem_iys, sem_iyr, sem_gxs, sem_gxr, sem_gys, sem_gyr,
    sem_ucs, sem_ucr, sem_uzs, sem_uzr, sem_uys, sem_uyr,
    sem_1s, sem_1r, sem_2s, sem_2r, sem_g1s, sem_g1r, sem_g2s, sem_g2r,
):
    u = lax.axis_index("user")
    j = lax.axis_index("item")
    z, yh, c = u // 4, (u // 2) % 2, u % 2
    yl, x = j // 4, j % 4

    def at_z(d):
        return (((z + d + 8) % 8) * 4 + yh * 2 + c, j)

    def at_x(d):
        return (u, yl * 4 + (x + d + 4) % 4)

    def at_zy(d):
        return (((z + d + 8) % 8) * 4 + (1 - yh) * 2 + c, j)

    y_user = (z * 4 + (1 - yh) * 2 + c, j)
    core = (z * 4 + yh * 2 + 1 - c, j)
    y_item = (u, (1 - yl) * 4 + x)

    def peer_u(k):
        return ((u + k) % 32, j)

    def peer_i(k):
        return (u, ((yl + k // 4) % 2) * 4 + (x + k % 4) % 4)

    sent = []

    def remote(src, dst, ssem, rsem, dev):
        return pltpu.make_async_remote_copy(
            src_ref=src, dst_ref=dst, send_sem=ssem, recv_sem=rsem, device_id=dev, device_id_type=MESH
        )

    def send(src, dst, ssem, rsem, dev):
        copy = remote(src, dst, ssem, rsem, dev)
        copy.start()
        sent.append(copy)

    def recv(dst, ssem, rsem, dev):
        remote(dst, dst, ssem, rsem, dev).wait_recv()

    barrier = pltpu.get_barrier_semaphore()
    near_devices = [at_z(1), at_z(-1), at_z(2), at_z(-2)]
    near_devices += [at_x(1), at_x(-1), y_user, y_item, core]
    for dev in near_devices:
        pl.semaphore_signal(barrier, inc=1, device_id=dev, device_id_type=MESH)

    rows = pl.ds(pl.multiple_of(j * 256, 256), 256)
    local = [
        pltpu.make_async_copy(w_hbm, w, sem_loc.at[1]),
        pltpu.make_async_copy(lvl_hbm, lvl, sem_loc.at[0]),
        pltpu.make_async_copy(uf_hbm.at[rows], uf, sem_loc.at[2]),
        pltpu.make_async_copy(ct_hbm.at[rows], ct, sem_loc.at[3]),
    ]
    for copy in local:
        copy.start()

    spot = lax.broadcasted_iota(jnp.int32, (8, 128), 0) * 128 + lax.broadcasted_iota(jnp.int32, (8, 128), 1)

    def place_slot(s, table):
        key = jnp.where(s < count_ref[0, 0], place_ref[s], -1)
        return jnp.where(spot == key, s, table)

    tab[...] = lax.fori_loop(0, 80, place_slot, jnp.full((8, 128), -1, jnp.int32))
    table_copy = pltpu.make_async_copy(tab, tabs, sem_loc.at[4])
    table_copy.start()

    cats = (cat_ref[...] - j * 4).astype(F32)
    cats = jnp.broadcast_to(jnp.concatenate([cats, cats], axis=1), (8, 128))
    catr[u] = cats
    col = jnp.transpose(cats)[0:64, 0:1]
    feats = x_ref[...].astype(F32)
    xg[z, yh * 2 + c] = x_ref[...]
    local[0].wait()
    total = jnp.zeros((64, 512), F32)
    for expert in range(4):
        masked = jnp.where(col == float(expert), feats, 0.0).astype(BF16)
        total = total + jnp.dot(masked, w[expert], preferred_element_type=F32)
    for fh in range(2):
        qg[fh, z, yh * 2 + c] = total[:, fh * 256 : fh * 256 + 256].astype(BF16)

    def hops(d, k):
        return 4 if (k == 0) == (d == R) else 3

    class Gather:
        def __init__(self, buf, sems):
            self.buf, self.sems = buf, sems

        def block(self, d, k, cc):
            return self.buf.at[(z + d + 8) % 8, (yh if k == 0 else 1 - yh) * 2 + cc]

        def pair(self, n):
            return self.sems.at[0, n], self.sems.at[1, n]

        def put(self, d, k, n, dev):
            block = self.block(d, k, c)
            send(block, block, *self.pair(n), dev)

        def out(self, k):
            for dist in (2, 1):
                for d in (R, L):
                    self.put(0, k, (d * 2 + k) * 4 + dist - 1, at_z(DIR[d] * dist))
            self.put(0, k, 16 + k, core)

        def begin(self):
            self.put(0, 0, 32, y_user)
            self.out(0)

        def cross(self):
            recv(self.block(0, 1, c), *self.pair(32), y_user)
            self.out(1)

        def take(self, k, dist):
            for d in (R, L):
                if dist > hops(d, k):
                    continue
                off, n = -DIR[d] * dist, (d * 2 + k) * 4
                recv(self.block(off, k, c), *self.pair(n + dist - 1), at_z(off))
                if dist == 2:
                    if hops(d, k) == 4:
                        self.put(off, k, n + 3, at_z(2 * DIR[d]))
                    self.put(off, k, n + 2, at_z(DIR[d]))
                self.put(off, k, 16 + (off % 8) * 2 + k, core)

        def near(self, k):
            self.take(k, 2)
            self.take(k, 1)

        def far(self, k):
            self.take(k, 3)
            self.take(k, 4)

        def settle(self, d):
            for k in range(2):
                recv(self.block(d, k, 1 - c), *self.pair(16 + (d % 8) * 2 + k), core)

    queries = [Gather(qg.at[fh], sem_q.at[fh]) for fh in range(2)]
    items = Gather(xg, sem_f)

    def build(zs):
        def body(rb, _):
            for half in range(2):
                pos = rb * 16 + zs * 2 + half
                slot = tabs[pos // 128, pos % 128]
                scale = jnp.where(slot >= 0, 1.0 / 256, 0.0)
                tile = lvl[jnp.maximum(slot, 0)].astype(F32) * scale
                col0 = zs * 256 + half * 128
                amat[pl.ds(pl.multiple_of(rb * 128, 128), 128), col0 : col0 + 128] = tile.astype(BF16)
            return 0

        lax.fori_loop(0, 16, body, 0)

    def ihops(d, h):
        return 2 if (h == 0) == (d == R) else 1

    def jat(dx, y):
        return y * 4 + (x + dx + 4) % 4

    def ysel(k):
        return 1 - yl if k == 0 else yl

    def product(fh, dx, k):
        jt = jat(dx, ysel(k))
        part = jnp.dot(
            amat[pl.ds(pl.multiple_of(jt * 256, 256), 256), :],
            qg[fh].reshape(2048, 256),
            preferred_element_type=F32,
        )
        acc[fh, pl.ds(jt * 2, 2)] = part.reshape(2, 128, 256)

    def term(fh, dx, k, h):
        return acc[fh, jat(dx, ysel(k)) * 2 + h]

    def mx_send(fh, d, k, h, s, value):
        n = (fh, d, k, h, s)
        mxs[n] = value.astype(BF16)
        send(mxs.at[n], mxr.at[n], sem_ixs.at[n], sem_ixr.at[n], at_x(DIR[d]))

    def mx_recv(fh, d, k, h, s):
        n = (fh, d, k, h, s)
        recv(mxr.at[n], sem_ixs.at[n], sem_ixr.at[n], at_x(-DIR[d]))
        return mxr[n].astype(F32)

    combos = [(d, h) for d in (R, L) for h in range(2)]

    def far(fh, k):
        for d, h in combos:
            if ihops(d, h) == 2:
                mx_send(fh, d, k, h, 1, term(fh, 2, k, h))

    def near(fh, k):
        for d, h in combos:
            if ihops(d, h) == 1:
                mx_send(fh, d, k, h, 0, term(fh, DIR[d], k, h))

    def relay(fh, k):
        for d, h in combos:
            if ihops(d, h) == 2:
                mx_send(fh, d, k, h, 0, term(fh, DIR[d], k, h) + mx_recv(fh, d, k, h, 1))

    def pair_put(slot, h, value):
        n = (slot, h)
        mys[n] = value.astype(BF16)
        send(mys.at[n], myr.at[n], sem_iys.at[n], sem_iyr.at[n], y_item)

    def pair_take(slot, h):
        n = (slot, h)
        recv(myr.at[n], sem_iys.at[n], sem_iyr.at[n], y_item)
        return myr[n].astype(F32)

    PAIR = {2: 1, 1: 2, -1: 3, 0: 4}

    def pair_last():
        for h in range(2):
            pair_put(0, h, term(0, 0, 0, h) + mx_recv(0, R, 0, h, 0) + mx_recv(0, L, 0, h, 0))

    def pair_first(dx):
        product(1, dx, 0)
        for h in range(2):
            pair_put(PAIR[dx], h, term(1, dx, 0, h))

    def pair_add(dx):
        for h in range(2):
            n = jat(dx, yl) * 2 + h
            acc[1, n] = acc[1, n] + pair_take(PAIR[dx], h)

    def summed(fh, h):
        value = term(fh, 0, 1, h) + mx_recv(fh, R, 1, h, 0) + mx_recv(fh, L, 1, h, 0)
        return value + pair_take(0, h) if fh == 0 else value

    def cats_start(k, _):
        remote(catr.at[u], catr.at[u], sem_cs.at[k], sem_cr.at[k], peer_u(k)).start()
        return 0

    def cats_wait(k, _):
        src = catr.at[(u + 32 - k) % 32]
        remote(src, src, sem_cs.at[k], sem_cr.at[k], peer_u(k)).wait()
        return 0

    low = lax.broadcasted_iota(jnp.int32, (8, 128), 1) < 64

    def cats_pair(p, _):
        catl[p] = jnp.where(low, catr[p * 2], catr[p * 2 + 1])
        return 0

    def all_here(fh):
        for d in range(-3, 5):
            queries[fh].settle(d)

    pl.semaphore_wait(barrier, 9)
    queries[0].begin()
    queries[1].begin()
    local[1].wait()
    table_copy.wait()
    for zs in range(4):
        build(zs)
    queries[0].cross()
    queries[0].near(0)
    queries[1].cross()
    queries[1].near(0)
    for zs in range(4, 8):
        build(zs)
    queries[0].near(1)
    queries[0].far(0)
    queries[1].near(1)
    queries[1].far(0)
    queries[0].far(1)
    all_here(0)
    for k in range(2):
        product(0, 2, k)
        far(0, k)
    for k in range(2):
        product(0, 1, k)
        product(0, -1, k)
        near(0, k)
    queries[1].far(1)
    all_here(1)
    for dx in (2, 1, -1, 0):
        pair_first(dx)
    product(0, 0, 0)
    product(0, 0, 1)
    items.begin()
    product(1, 2, 1)
    relay(0, 0)
    relay(0, 1)
    product(1, 1, 1)
    product(1, -1, 1)
    product(1, 0, 1)
    pair_add(2)
    far(1, 1)
    pair_last()
    pair_add(1)
    pair_add(-1)
    near(1, 1)
    relay(1, 1)
    lax.fori_loop(1, 32, cats_start, 0)
    pair_add(0)

    local[2].wait()
    local[3].wait()
    gain = [gain_ref[:, fh * 256 : fh * 256 + 256] for fh in range(2)]
    gsum = [jnp.zeros((1, 256), F32) for fh in range(2)]

    def g_cross_start(fh, h):
        block = ugall.at[fh, j, h]
        send(block, block, sem_gys.at[fh, h], sem_gyr.at[fh, h], y_item)

    def g_ring_start(fh, h, k):
        for d in (R, L):
            block = ugall.at[fh, jat(0, yl if k == 0 else 1 - yl), h]
            send(block, block, sem_gxs.at[fh, d, k, h, 0], sem_gxr.at[fh, d, k, h, 0], at_x(DIR[d]))

    def g_cross(fh):
        for h in range(2):
            recv(ugall.at[fh, jat(0, 1 - yl), h], sem_gys.at[fh, h], sem_gyr.at[fh, h], y_item)
            if fh == 0:
                g_ring_start(fh, h, 1)

    def g_step(fh, k, s):
        y = yl if k == 0 else 1 - yl
        for h in range(2):
            for d in (R, L):
                if s > ihops(d, h):
                    continue
                block = ugall.at[fh, jat(-DIR[d] * s, y), h]
                n = (fh, d, k, h, s - 1)
                recv(block, sem_gxs.at[n], sem_gxr.at[n], at_x(-DIR[d]))
                if s < ihops(d, h) and (fh == 0 or k == 0):
                    n = (fh, d, k, h, s)
                    send(block, block, sem_gxs.at[n], sem_gxr.at[n], at_x(DIR[d]))
                if fh == 1 and k == 0:
                    n = (fh, d, 1, h, s - 1)
                    send(block, block, sem_gxs.at[n], sem_gxr.at[n], y_item)

    for h in range(2):
        feat_rows = slice(h * 128, h * 128 + 128)
        pre, grad = [], []
        for fh in range(2):
            cols = slice(fh * 256, fh * 256 + 256)
            pre.append(uf[feat_rows, cols].astype(F32) + summed(fh, h))
            grad.append(ct[feat_rows, cols].astype(F32))
        squares = sum(jnp.sum(p * p, axis=-1, keepdims=True) for p in pre)
        crossed = sum(jnp.sum(gain[fh] * grad[fh] * pre[fh], axis=-1, keepdims=True) for fh in range(2))
        inv = lax.rsqrt(squares * (1.0 / 512) + 1e-05)
        factor = inv * inv * inv * (crossed * (1.0 / 512))
        for fh in range(2):
            ugall[fh, j, h] = (inv * (gain[fh] * grad[fh]) - factor * pre[fh]).astype(BF16)
            gsum[fh] = gsum[fh] + jnp.sum(grad[fh] * pre[fh] * inv, axis=0, keepdims=True)
        g_cross_start(0, h)
        g_ring_start(0, h, 0)
    for h in range(2):
        g_cross_start(1, h)
        g_ring_start(1, h, 0)
    gs[...] = jnp.zeros((8, 128), F32)
    for t in range(4):
        gs[t : t + 1, :] = gsum[t // 2][:, (t % 2) * 128 : (t % 2) * 128 + 128]

    def gain_i(k, _):
        remote(gs, gr.at[k], sem_g1s.at[k], sem_g1r.at[k], peer_i(k)).start()
        return 0

    lax.fori_loop(1, 8, gain_i, 0)

    def back(fh, dx, y, first=False):
        jj = jat(dx, y)
        ugt[...] = jnp.transpose(ugall[fh, jj].reshape(256, 256).astype(F32)).astype(BF16)
        for zs in range(8):
            part = jnp.dot(
                ugt[...],
                amat[pl.ds(pl.multiple_of(jj * 256, 256), 256), zs * 256 : zs * 256 + 256],
                preferred_element_type=F32,
            )
            acc2[fh, zs] = part if first else acc2[fh, zs] + part

        @pl.when(j // 4 == fh)
        def _():
            ug_out[:, pl.ds(pl.multiple_of(jj * 256, 256), 256)] = ugt[
                pl.ds(pl.multiple_of((j % 4) * 64, 64), 64), :
            ]

    def piece(fh, zs, y, cc):
        v = acc2[fh, :, pl.ds(pl.multiple_of((zs * 4 + y * 2 + cc) * 8, 8), 8), :]
        return jnp.concatenate([v[0:4], v[4:8]], axis=1)

    def core_start(fh):
        for d in (4, 3, -3, 1, -1, 2, -2, 0):
            zs = (z + d + 8) % 8
            for y in range(2):
                cs[fh, zs, y] = piece(fh, zs, y, 1 - c).astype(BF16)
            send(cs.at[fh, zs], cr.at[fh, zs], sem_ucs.at[fh, d % 8], sem_ucr.at[fh, d % 8], core)

    def core_recv(fh, d):
        recv(cr.at[fh, (z + d + 8) % 8], sem_ucs.at[fh, d % 8], sem_ucr.at[fh, d % 8], core)

    def own_sum(fh, d, y):
        zs = (z + d + 8) % 8
        return piece(fh, zs, y, c) + cr[fh, zs, y].astype(F32)

    def z_send(fh, d, k, slot, value, dist):
        n = (fh, d, k, slot)
        rs[n] = value.astype(BF16)
        dev = at_zy(DIR[d] * dist) if k == 0 and slot < 2 else at_z(DIR[d] * dist)
        send(rs.at[n], rr.at[n], sem_uzs.at[n], sem_uzr.at[n], dev)

    def z_recv(fh, d, k, slot):
        n = (fh, d, k, slot)
        recv(rr.at[n], sem_uzs.at[n], sem_uzr.at[n], at_z(-DIR[d]))
        return rr[n].astype(F32)

    def uy(k):
        return 1 - yh if k == 0 else yh

    ucombos = [(k, d) for k in range(2) for d in (R, L)]

    def u_out(fh):
        core_recv(fh, 4)
        for k, d in ucombos:
            if hops(d, k) == 4:
                z_send(fh, d, k, 3, own_sum(fh, 4, uy(k)), 2)
        for dist, slot in ((3, 2), (1, 0)):
            core_recv(fh, dist)
            core_recv(fh, -dist)
            for k, d in ucombos:
                z_send(fh, d, k, slot, own_sum(fh, DIR[d] * dist, uy(k)), 1)

    def u_mid(fh):
        core_recv(fh, 2)
        core_recv(fh, -2)
        for k, d in ucombos:
            value = own_sum(fh, DIR[d] * 2, uy(k)) + z_recv(fh, d, k, 2)
            if hops(d, k) == 4:
                value = value + z_recv(fh, d, k, 3)
            z_send(fh, d, k, 1, value, 2)

    def u_cross(fh):
        core_recv(fh, 0)
        ys[fh] = own_sum(fh, 0, 1 - yh).astype(BF16)
        send(ys.at[fh], yr.at[fh], sem_uys.at[fh], sem_uyr.at[fh], y_user)

    def u_final(fh):
        mine = own_sum(fh, 0, yh)
        for k, d in ucombos:
            mine = mine + z_recv(fh, d, k, 0) + z_recv(fh, d, k, 1)
        recv(yr.at[fh], sem_uys.at[fh], sem_uyr.at[fh], y_user)
        return mine + yr[fh].astype(F32)

    back(0, 0, yl, True)
    items.cross()
    back(1, 0, yl, True)
    g_cross(0)
    g_step(0, 0, 1)
    g_step(1, 0, 1)
    back(0, 1, yl)
    back(0, -1, yl)
    items.near(0)
    g_cross(1)
    back(0, 0, 1 - yl)
    back(1, 1, yl)
    g_step(0, 1, 1)
    back(0, 1, 1 - yl)
    g_step(0, 0, 2)
    back(0, 2, yl)
    g_step(1, 0, 2)
    back(0, -1, 1 - yl)
    g_step(0, 1, 2)
    back(0, 2, 1 - yl)
    core_start(0)
    back(1, -1, yl)
    back(1, 0, 1 - yl)
    items.near(1)
    items.far(0)
    u_cross(0)
    u_out(0)
    g_step(1, 1, 1)
    back(1, 2, yl)
    back(1, 1, 1 - yl)
    back(1, -1, 1 - yl)
    g_step(1, 1, 2)
    back(1, 2, 1 - yl)
    core_start(1)
    items.far(1)
    u_cross(1)
    u_out(1)
    u_mid(0)

    def gain_i_wait(k, total):
        remote(gs, gr.at[k], sem_g1s.at[k], sem_g1r.at[k], peer_i(k)).wait()
        return total + gr[k]

    gt[...] = lax.fori_loop(1, 8, gain_i_wait, gs[...])

    def gain_u(k, _):
        remote(gt, gr2.at[k], sem_g2s.at[k], sem_g2r.at[k], peer_u(k)).start()
        return 0

    lax.fori_loop(1, 32, gain_u, 0)
    u_mid(1)
    lax.fori_loop(1, 32, cats_wait, 0)
    lax.fori_loop(0, 16, cats_pair, 0)
    for d in range(-3, 5):
        items.settle(d)
    mine = jnp.concatenate(
        [
            jnp.concatenate([value[:, 0:8], value[:, 8:16]], axis=0)
            for value in (u_final(0), u_final(1))
        ],
        axis=1,
    ).astype(BF16)
    for zs in range(8):
        for half in range(2):
            sumb[zs * 2 + half] = mine[zs, :, half * 128 : half * 128 + 128]

    st[u] = sumb[u // 2]

    def sums_start(k, _):
        remote(sumb.at[((u + k) % 32) // 2], st.at[u], sem_1s.at[k], sem_1r.at[k], peer_u(k)).start()
        return 0

    lax.fori_loop(1, 32, sums_start, 0)

    for p in range(16):
        cat16 = jnp.concatenate([catl[p], catl[p]], axis=0)
        value = sumb[p].astype(F32)
        for expert in range(4):
            ms[expert * 16 : expert * 16 + 16, p * 128 : p * 128 + 128] = jnp.where(
                cat16 == float(expert), value, 0.0
            ).astype(BF16)
    grads = jnp.zeros((64, 512), F32)
    for zs in range(8):
        grads = grads + jnp.dot(
            ms[:, zs * 256 : zs * 256 + 256], xg[zs].reshape(256, 512), preferred_element_type=F32
        )
    wide = jnp.transpose(jnp.concatenate([grads, grads], axis=0)).reshape(32, 2, 8, 128)
    es[...] = jnp.where(low[None], wide[:, 0], wide[:, 1])
    er[u] = es[u]

    def grads_start(k, _):
        remote(es.at[(u + k) % 32], er.at[u], sem_2s.at[k], sem_2r.at[k], peer_u(k)).start()
        return 0

    lax.fori_loop(1, 32, grads_start, 0)

    def gain_u_wait(k, total):
        remote(gt, gr2.at[k], sem_g2s.at[k], sem_g2r.at[k], peer_u(k)).wait()
        return total + gr2[k]

    gs2 = lax.fori_loop(1, 32, gain_u_wait, gt[...])
    gr[0] = gs2
    grow = gr[0, pl.ds(j // 2, 1), :]
    gg_out[...] = jnp.where(j % 2 == 0, grow[:, 0:64], grow[:, 64:128])

    def sums_wait(k, _):
        dst = st.at[(u + 32 - k) % 32]
        remote(dst, dst, sem_1s.at[k], sem_1r.at[k], peer_u(k)).wait()
        return 0

    lax.fori_loop(1, 32, sums_wait, 0)
    wide = st[...].astype(F32)
    sums = jnp.concatenate([wide[:, 0:8], wide[:, 8:16]], axis=0).reshape(512, 128)
    cat1 = catl[u // 2][0:1, :]
    total = jnp.zeros((512, 128), F32)
    for expert in range(4):
        masked = jnp.where(cat1 == float(expert), sums, 0.0).astype(BF16)
        total = total + jnp.dot(w[expert], masked, preferred_element_type=F32)
    igt[...] = jnp.transpose(total)
    ig_out[...] = igt[pl.ds(pl.multiple_of(c * 64, 64), 64), :].astype(BF16)

    def grads_wait(k, _):
        dst = er.at[(u + 32 - k) % 32]
        remote(dst, dst, sem_2s.at[k], sem_2r.at[k], peer_u(k)).wait()
        return 0

    lax.fori_loop(1, 32, grads_wait, 0)
    lane = lax.broadcasted_iota(jnp.int32, (8, 128), 1) // 8
    for expert in range(4):
        for half in range(2):
            for t in range(4):
                line = jnp.zeros((8, 128), F32)
                for k in range(16):
                    shift = k * 8 - half * 64 - expert * 16 - (t // 2) * 8
                    moved = pltpu.roll(er[(t % 2) * 16 + k], shift % 128, 1)
                    line = jnp.where(lane == k, moved, line)
                eg_out[expert, half * 8 : half * 8 + 8, t * 128 : t * 128 + 128] = line

    for copy in sent:
        copy.wait_send()


def settle(ug, ig, eg, gg, ug_out, ig_out, eg_out, gg_out):
    for src, dst in ((ug, ug_out), (ig, ig_out), (eg, eg_out), (gg, gg_out)):
        dst[...] = src[...]


def on_device(
    user_feat, cotangent, gain, item_feat, categories, expert_w, tile_place, tile_level, tile_count
):
    vmem = pl.BlockSpec(memory_space=pltpu.VMEM)
    smem = pl.BlockSpec(memory_space=pltpu.SMEM)
    hbm = pl.BlockSpec(memory_space=pl.ANY)
    V = pltpu.VMEM
    scratch = [
        V((8, 4, 64, 512), BF16), V((2, 8, 4, 64, 256), BF16), V((4, 512, 512), BF16), V((80, 128, 128), jnp.int32),
        V((2048, 2048), BF16), V((2, 16, 128, 256), F32),
        V((256, 512), BF16), V((256, 512), BF16), V((32, 8, 128), F32), V((16, 8, 128), F32),
        V((8, 128), jnp.int32), pltpu.SMEM((8, 128), jnp.int32),
        V((2, 2, 2, 2, 2, 128, 256), BF16), V((2, 2, 2, 2, 2, 128, 256), BF16),
        V((5, 2, 128, 256), BF16), V((5, 2, 128, 256), BF16),
        V((2, 8, 2, 128, 256), BF16), V((256, 256), BF16), V((2, 8, 256, 256), F32),
        V((2, 8, 2, 4, 16, 256), BF16), V((2, 8, 2, 4, 16, 256), BF16),
        V((2, 2, 2, 4, 4, 16, 256), BF16), V((2, 2, 2, 4, 4, 16, 256), BF16),
        V((2, 4, 16, 256), BF16), V((2, 4, 16, 256), BF16),
        V((16, 16, 128), BF16), V((32, 16, 128), BF16), V((64, 2048), BF16),
        V((32, 8, 128), F32), V((32, 8, 128), F32), V((128, 512), F32),
        V((8, 128), F32), V((8, 8, 128), F32), V((8, 128), F32), V((32, 8, 128), F32),
        DMA((5,)), DMA((32,)), DMA((32,)), DMA((2, 2, 33)), DMA((2, 33)),
        DMA((2, 2, 2, 2, 2)), DMA((2, 2, 2, 2, 2)), DMA((5, 2)), DMA((5, 2)),
        DMA((2, 2, 2, 2, 2)), DMA((2, 2, 2, 2, 2)), DMA((2, 2)), DMA((2, 2)),
        DMA((2, 8)), DMA((2, 8)), DMA((2, 2, 2, 4)), DMA((2, 2, 2, 4)), DMA((2,)), DMA((2,)),
        DMA((32,)), DMA((32,)), DMA((32,)), DMA((32,)), DMA((8,)), DMA((8,)), DMA((32,)), DMA((32,)),
    ]
    shapes = (
        jax.ShapeDtypeStruct((64, 2048), BF16),
        jax.ShapeDtypeStruct((64, 512), BF16),
        jax.ShapeDtypeStruct((4, 16, 512), F32),
        jax.ShapeDtypeStruct((1, 64), F32),
    )
    parts = pl.pallas_call(
        layer,
        out_shape=shapes,
        in_specs=[vmem, vmem, vmem, smem, smem, hbm, hbm, hbm, hbm],
        out_specs=(vmem, vmem, vmem, vmem),
        scratch_shapes=scratch,
        compiler_params=pltpu.CompilerParams(
            collective_id=0, has_side_effects=True, vmem_limit_bytes=60 * 2**20
        ),
    )(
        item_feat[0], categories, gain[None, :], tile_place[0, 0], tile_count, expert_w, tile_level[0, 0],
        user_feat, cotangent,
    )
    ug, ig, eg, gg = pl.pallas_call(
        settle,
        out_shape=shapes,
        in_specs=[vmem] * 4,
        out_specs=(vmem,) * 4,
    )(*parts)
    return ug.T, ig[None], eg, gg[0]


def solution(mesh):
    placed = (
        P("user", None),
        P("user", None),
        P(),
        P("item", "user", None),
        P("item", "user"),
        P("item", None, None),
        P("user", "item", None),
        P("user", "item", None, None, None),
        P("user", "item"),
    )
    return jax.shard_map(
        on_device,
        mesh=mesh,
        in_specs=placed,
        out_specs=(P("user", "item"), P("item", "user", None), P("item", "user", None), P("item")),
        check_vma=False,
    )
```

```python
import jax
import jax.numpy as jnp
from jax import lax
from jax.experimental import pallas as pl
from jax.experimental.pallas import tpu as pltpu
from jax.sharding import PartitionSpec as P

MESH = pl.DeviceIdType.MESH
F32 = jnp.float32
BF16 = jnp.bfloat16
DMA = pltpu.SemaphoreType.DMA
R, L = 0, 1
DIR = (1, -1)


def layer(
    x_ref, cat_ref, gain_ref, place_ref, count_ref, w_hbm, lvl_hbm, uf_hbm, ct_hbm,
    ug_out, ig_out, eg_out, gg_out,
    xg, qg, w, lvl, amat, acc, uf, ct, catl, tab, tabs,
    mxs, mxr, mys, myr, ugall, ugt, acc2,
    cs, cr, rs, rr, ys, yr, sumb, st, ms, es, er, igt, gs, gr, gt, gr2,
    sem_loc, sem_q, sem_f,
    sem_ixs, sem_ixr, sem_iys, sem_iyr, sem_gxs, sem_gxr, sem_gys, sem_gyr,
    sem_ucs, sem_ucr, sem_uzs, sem_uzr, sem_uys, sem_uyr,
    sem_1s, sem_1r, sem_2s, sem_2r, sem_g1s, sem_g1r, sem_g2s, sem_g2r,
):
    u = lax.axis_index("user")
    j = lax.axis_index("item")
    z, yh, c = u // 4, (u // 2) % 2, u % 2
    yl, x = j // 4, j % 4

    def at_z(d):
        return (((z + d + 8) % 8) * 4 + yh * 2 + c, j)

    def at_x(d):
        return (u, yl * 4 + (x + d + 4) % 4)

    def at_zy(d):
        return (((z + d + 8) % 8) * 4 + (1 - yh) * 2 + c, j)

    y_user = (z * 4 + (1 - yh) * 2 + c, j)
    core = (z * 4 + yh * 2 + 1 - c, j)
    y_item = (u, (1 - yl) * 4 + x)

    def peer_u(k):
        return ((u + k) % 32, j)

    def peer_i(k):
        return (u, ((yl + k // 4) % 2) * 4 + (x + k % 4) % 4)

    sent = []

    def remote(src, dst, ssem, rsem, dev):
        return pltpu.make_async_remote_copy(
            src_ref=src, dst_ref=dst, send_sem=ssem, recv_sem=rsem, device_id=dev, device_id_type=MESH
        )

    def send(src, dst, ssem, rsem, dev):
        copy = remote(src, dst, ssem, rsem, dev)
        copy.start()
        sent.append(copy)

    def recv(dst, ssem, rsem, dev):
        remote(dst, dst, ssem, rsem, dev).wait_recv()

    barrier = pltpu.get_barrier_semaphore()
    near_devices = [at_z(1), at_z(-1), at_z(2), at_z(-2)]
    near_devices += [at_x(1), at_x(-1), y_user, y_item, core]
    for dev in near_devices:
        pl.semaphore_signal(barrier, inc=1, device_id=dev, device_id_type=MESH)

    rows = pl.ds(pl.multiple_of(j * 256, 256), 256)
    local = [
        pltpu.make_async_copy(w_hbm, w, sem_loc.at[1]),
        pltpu.make_async_copy(lvl_hbm, lvl, sem_loc.at[0]),
        pltpu.make_async_copy(uf_hbm.at[rows], uf, sem_loc.at[2]),
        pltpu.make_async_copy(ct_hbm.at[rows], ct, sem_loc.at[3]),
    ]
    for copy in local:
        copy.start()

    spot = lax.broadcasted_iota(jnp.int32, (8, 128), 0) * 128 + lax.broadcasted_iota(jnp.int32, (8, 128), 1)

    def place_slot(s, table):
        key = jnp.where(s < count_ref[0, 0], place_ref[s], -1)
        return jnp.where(spot == key, s, table)

    tab[...] = lax.fori_loop(0, 80, place_slot, jnp.full((8, 128), -1, jnp.int32))
    table_copy = pltpu.make_async_copy(tab, tabs, sem_loc.at[4])
    table_copy.start()

    cats = (cat_ref[...] - j * 4).astype(F32)
    cats = jnp.broadcast_to(jnp.concatenate([cats, cats], axis=1), (8, 128))
    col = jnp.transpose(cats)[0:64, 0:1]
    feats = x_ref[...].astype(F32)
    xg[z, yh * 2 + c] = x_ref[...]
    local[0].wait()
    total = jnp.zeros((64, 512), F32)
    for expert in range(4):
        masked = jnp.where(col == float(expert), feats, 0.0).astype(BF16)
        total = total + jnp.dot(masked, w[expert], preferred_element_type=F32)
    for fh in range(2):
        qg[fh, z, yh * 2 + c] = total[:, fh * 256 : fh * 256 + 256].astype(BF16)

    def hops(d, k):
        return 4 if (k == 0) == (d == R) else 3

    class Gather:
        def __init__(self, buf, sems, late=False):
            self.buf, self.sems, self.late = buf, sems, late

        def hops(self, d, k):
            return hops(d, 0 if self.late else k)

        def block(self, d, k, cc):
            return self.buf.at[(z + d + 8) % 8, (yh if k == 0 else 1 - yh) * 2 + cc]

        def pair(self, n):
            return self.sems.at[0, n], self.sems.at[1, n]

        def put(self, d, k, n, dev):
            block = self.block(d, k, c)
            send(block, block, *self.pair(n), dev)

        def out(self, k):
            for dist in (2, 1):
                for d in (R, L):
                    self.put(0, k, (d * 2 + k) * 4 + dist - 1, at_z(DIR[d] * dist))
            self.put(0, k, 16 + k, core)

        def begin(self):
            self.put(0, 0, 32, y_user)
            self.out(0)

        def cross(self):
            recv(self.block(0, 1, c), *self.pair(32), y_user)
            if self.late:
                self.put(0, 1, 17, core)
            else:
                self.out(1)

        def take(self, k, dist):
            for d in (R, L):
                if dist > self.hops(d, k):
                    continue
                off, n = -DIR[d] * dist, (d * 2 + k) * 4
                recv(self.block(off, k, c), *self.pair(n + dist - 1), at_z(off))
                if dist == 2 and not (self.late and k == 1):
                    if self.hops(d, k) == 4:
                        self.put(off, k, n + 3, at_z(2 * DIR[d]))
                    self.put(off, k, n + 2, at_z(DIR[d]))
                if self.late and k == 0:
                    self.put(off, 0, (d * 2 + 1) * 4 + dist - 1, y_user)
                self.put(off, k, 16 + (off % 8) * 2 + k, core)

        def near(self, k):
            self.take(k, 2)
            self.take(k, 1)

        def far(self, k):
            self.take(k, 3)
            self.take(k, 4)

        def settle(self, d):
            for k in range(2):
                recv(self.block(d, k, 1 - c), *self.pair(16 + (d % 8) * 2 + k), core)

    queries = [Gather(qg.at[fh], sem_q.at[fh], fh == 1) for fh in range(2)]
    items = Gather(xg, sem_f)

    def build(zs):
        def body(rb, _):
            for half in range(2):
                pos = rb * 16 + zs * 2 + half
                slot = tabs[pos // 128, pos % 128]
                scale = jnp.where(slot >= 0, 1.0 / 256, 0.0)
                tile = lvl[jnp.maximum(slot, 0)].astype(F32) * scale
                col0 = zs * 256 + half * 128
                amat[pl.ds(pl.multiple_of(rb * 128, 128), 128), col0 : col0 + 128] = tile.astype(BF16)
            return 0

        lax.fori_loop(0, 16, body, 0)

    def ihops(d, h):
        return 2 if (h == 0) == (d == R) else 1

    def jat(dx, y):
        return y * 4 + (x + dx + 4) % 4

    def ysel(k):
        return 1 - yl if k == 0 else yl

    def product(fh, dx, k):
        jt = jat(dx, ysel(k))
        part = jnp.dot(
            amat[pl.ds(pl.multiple_of(jt * 256, 256), 256), :],
            qg[fh].reshape(2048, 256),
            preferred_element_type=F32,
        )
        acc[fh, pl.ds(jt * 2, 2)] = part.reshape(2, 128, 256)

    def term(fh, dx, k, h):
        return acc[fh, jat(dx, ysel(k)) * 2 + h]

    def mx_send(fh, d, k, h, s, value):
        n = (fh, d, k, h, s)
        mxs[n] = value.astype(BF16)
        send(mxs.at[n], mxr.at[n], sem_ixs.at[n], sem_ixr.at[n], at_x(DIR[d]))

    def mx_recv(fh, d, k, h, s):
        n = (fh, d, k, h, s)
        recv(mxr.at[n], sem_ixs.at[n], sem_ixr.at[n], at_x(-DIR[d]))
        return mxr[n].astype(F32)

    combos = [(d, h) for d in (R, L) for h in range(2)]

    def far(fh, k):
        for d, h in combos:
            if ihops(d, h) == 2:
                mx_send(fh, d, k, h, 1, term(fh, 2, k, h))

    def near(fh, k):
        for d, h in combos:
            if ihops(d, h) == 1:
                mx_send(fh, d, k, h, 0, term(fh, DIR[d], k, h))

    def relay(fh, k):
        for d, h in combos:
            if ihops(d, h) == 2:
                mx_send(fh, d, k, h, 0, term(fh, DIR[d], k, h) + mx_recv(fh, d, k, h, 1))

    def pair_put(slot, h, value):
        n = (slot, h)
        mys[n] = value.astype(BF16)
        send(mys.at[n], myr.at[n], sem_iys.at[n], sem_iyr.at[n], y_item)

    def pair_take(slot, h):
        n = (slot, h)
        recv(myr.at[n], sem_iys.at[n], sem_iyr.at[n], y_item)
        return myr[n].astype(F32)

    PAIR = {2: 1, 1: 2, -1: 3, 0: 4}

    def pair_last():
        for h in range(2):
            pair_put(0, h, term(0, 0, 0, h) + mx_recv(0, R, 0, h, 0) + mx_recv(0, L, 0, h, 0))

    def pair_first(dx):
        product(1, dx, 0)
        for h in range(2):
            pair_put(PAIR[dx], h, term(1, dx, 0, h))

    def pair_add(dx):
        for h in range(2):
            n = jat(dx, yl) * 2 + h
            acc[1, n] = acc[1, n] + pair_take(PAIR[dx], h)

    def summed(fh, h):
        value = term(fh, 0, 1, h) + mx_recv(fh, R, 1, h, 0) + mx_recv(fh, L, 1, h, 0)
        return value + pair_take(0, h) if fh == 0 else value

    def all_here(fh):
        for d in range(-3, 5):
            queries[fh].settle(d)

    pl.semaphore_wait(barrier, 9)
    queries[0].begin()
    queries[1].begin()
    local[1].wait()
    table_copy.wait()
    for zs in range(4):
        build(zs)
    queries[0].cross()
    queries[0].near(0)
    queries[1].cross()
    queries[1].near(0)
    for zs in range(4, 8):
        build(zs)
    queries[0].near(1)
    queries[0].far(0)
    queries[1].far(0)
    queries[1].near(1)
    queries[0].far(1)
    all_here(0)
    for k in range(2):
        product(0, 2, k)
        far(0, k)
    for k in range(2):
        product(0, 1, k)
        product(0, -1, k)
        near(0, k)
    queries[1].far(1)
    all_here(1)
    for dx in (2, 1, -1, 0):
        pair_first(dx)
    product(0, 0, 0)
    product(0, 0, 1)
    items.begin()
    product(1, 2, 1)
    relay(0, 0)
    relay(0, 1)
    product(1, 1, 1)
    product(1, -1, 1)
    product(1, 0, 1)
    pair_add(2)
    far(1, 1)
    pair_last()
    pair_add(1)
    pair_add(-1)
    near(1, 1)
    relay(1, 1)
    pair_add(0)

    local[2].wait()
    local[3].wait()
    gain = [gain_ref[:, fh * 256 : fh * 256 + 256] for fh in range(2)]
    gsum = [jnp.zeros((1, 256), F32) for fh in range(2)]

    def g_cross_start(fh, h):
        block = ugall.at[fh, j, h]
        send(block, block, sem_gys.at[fh, h], sem_gyr.at[fh, h], y_item)

    def g_ring_start(fh, h, k):
        for d in (R, L):
            block = ugall.at[fh, jat(0, yl if k == 0 else 1 - yl), h]
            send(block, block, sem_gxs.at[fh, d, k, h, 0], sem_gxr.at[fh, d, k, h, 0], at_x(DIR[d]))

    def g_cross(fh):
        for h in range(2):
            recv(ugall.at[fh, jat(0, 1 - yl), h], sem_gys.at[fh, h], sem_gyr.at[fh, h], y_item)
            if fh == 0:
                g_ring_start(fh, h, 1)

    def g_step(fh, k, s):
        y = yl if k == 0 else 1 - yl
        for h in range(2):
            for d in (R, L):
                if s > ihops(d, h):
                    continue
                block = ugall.at[fh, jat(-DIR[d] * s, y), h]
                n = (fh, d, k, h, s - 1)
                recv(block, sem_gxs.at[n], sem_gxr.at[n], at_x(-DIR[d]))
                if s < ihops(d, h) and (fh == 0 or k == 0):
                    n = (fh, d, k, h, s)
                    send(block, block, sem_gxs.at[n], sem_gxr.at[n], at_x(DIR[d]))
                if fh == 1 and k == 0:
                    n = (fh, d, 1, h, s - 1)
                    send(block, block, sem_gxs.at[n], sem_gxr.at[n], y_item)

    for h in range(2):
        feat_rows = slice(h * 128, h * 128 + 128)
        pre, grad = [], []
        for fh in range(2):
            cols = slice(fh * 256, fh * 256 + 256)
            pre.append(uf[feat_rows, cols].astype(F32) + summed(fh, h))
            grad.append(ct[feat_rows, cols].astype(F32))
        squares = sum(jnp.sum(p * p, axis=-1, keepdims=True) for p in pre)
        crossed = sum(jnp.sum(gain[fh] * grad[fh] * pre[fh], axis=-1, keepdims=True) for fh in range(2))
        inv = lax.rsqrt(squares * (1.0 / 512) + 1e-05)
        factor = inv * inv * inv * (crossed * (1.0 / 512))
        for fh in range(2):
            ugall[fh, j, h] = (inv * (gain[fh] * grad[fh]) - factor * pre[fh]).astype(BF16)
            gsum[fh] = gsum[fh] + jnp.sum(grad[fh] * pre[fh] * inv, axis=0, keepdims=True)
        g_cross_start(0, h)
        g_ring_start(0, h, 0)
    for h in range(2):
        g_cross_start(1, h)
        g_ring_start(1, h, 0)
    gs[...] = jnp.zeros((8, 128), F32)
    for t in range(4):
        gs[t : t + 1, :] = gsum[t // 2][:, (t % 2) * 128 : (t % 2) * 128 + 128]

    def gain_i(k, _):
        remote(gs, gr.at[k], sem_g1s.at[k], sem_g1r.at[k], peer_i(k)).start()
        return 0

    lax.fori_loop(1, 8, gain_i, 0)

    def back(fh, dx, y, first=False):
        jj = jat(dx, y)
        ugt[...] = jnp.transpose(ugall[fh, jj].reshape(256, 256).astype(F32)).astype(BF16)
        for zs in range(8):
            part = jnp.dot(
                ugt[...],
                amat[pl.ds(pl.multiple_of(jj * 256, 256), 256), zs * 256 : zs * 256 + 256],
                preferred_element_type=F32,
            )
            acc2[fh, zs] = part if first else acc2[fh, zs] + part

        @pl.when(j // 4 == fh)
        def _():
            ug_out[:, pl.ds(pl.multiple_of(jj * 256, 256), 256)] = ugt[
                pl.ds(pl.multiple_of((j % 4) * 64, 64), 64), :
            ]

    def piece(fh, zs, y, cc):
        v = acc2[fh, :, pl.ds(pl.multiple_of((zs * 4 + y * 2 + cc) * 8, 8), 8), :]
        return jnp.concatenate([v[0:4], v[4:8]], axis=1)

    def core_start(fh):
        for d in (4, 3, -3, 1, -1, 2, -2, 0):
            zs = (z + d + 8) % 8
            for y in range(2):
                cs[fh, zs, y] = piece(fh, zs, y, 1 - c).astype(BF16)
            send(cs.at[fh, zs], cr.at[fh, zs], sem_ucs.at[fh, d % 8], sem_ucr.at[fh, d % 8], core)

    def core_recv(fh, d):
        recv(cr.at[fh, (z + d + 8) % 8], sem_ucs.at[fh, d % 8], sem_ucr.at[fh, d % 8], core)

    def own_sum(fh, d, y):
        zs = (z + d + 8) % 8
        return piece(fh, zs, y, c) + cr[fh, zs, y].astype(F32)

    def z_send(fh, d, k, slot, value, dist):
        n = (fh, d, k, slot)
        rs[n] = value.astype(BF16)
        dev = at_zy(DIR[d] * dist) if k == 0 and slot < 2 else at_z(DIR[d] * dist)
        send(rs.at[n], rr.at[n], sem_uzs.at[n], sem_uzr.at[n], dev)

    def z_recv(fh, d, k, slot):
        n = (fh, d, k, slot)
        recv(rr.at[n], sem_uzs.at[n], sem_uzr.at[n], at_z(-DIR[d]))
        return rr[n].astype(F32)

    def uy(k):
        return 1 - yh if k == 0 else yh

    ucombos = [(k, d) for k in range(2) for d in (R, L)]

    def u_out(fh):
        core_recv(fh, 4)
        for k, d in ucombos:
            if hops(d, k) == 4:
                z_send(fh, d, k, 3, own_sum(fh, 4, uy(k)), 2)
        for dist, slot in ((3, 2), (1, 0)):
            core_recv(fh, dist)
            core_recv(fh, -dist)
            for k, d in ucombos:
                z_send(fh, d, k, slot, own_sum(fh, DIR[d] * dist, uy(k)), 1)

    def u_mid(fh):
        core_recv(fh, 2)
        core_recv(fh, -2)
        for k, d in ucombos:
            value = own_sum(fh, DIR[d] * 2, uy(k)) + z_recv(fh, d, k, 2)
            if hops(d, k) == 4:
                value = value + z_recv(fh, d, k, 3)
            z_send(fh, d, k, 1, value, 2)

    def u_cross(fh):
        core_recv(fh, 0)
        ys[fh] = own_sum(fh, 0, 1 - yh).astype(BF16)
        send(ys.at[fh], yr.at[fh], sem_uys.at[fh], sem_uyr.at[fh], y_user)

    def u_final(fh):
        mine = own_sum(fh, 0, yh)
        for k, d in ucombos:
            mine = mine + z_recv(fh, d, k, 0) + z_recv(fh, d, k, 1)
        recv(yr.at[fh], sem_uys.at[fh], sem_uyr.at[fh], y_user)
        return mine + yr[fh].astype(F32)

    back(0, 0, yl, True)
    items.cross()
    back(1, 0, yl, True)
    g_cross(0)
    g_step(0, 0, 1)
    g_step(1, 0, 1)
    back(0, 1, yl)
    back(0, -1, yl)
    items.near(0)
    g_cross(1)
    back(0, 0, 1 - yl)
    back(1, 1, yl)
    g_step(0, 1, 1)
    back(0, 1, 1 - yl)
    g_step(0, 0, 2)
    back(0, 2, yl)
    g_step(1, 0, 2)
    back(0, -1, 1 - yl)
    g_step(0, 1, 2)
    back(0, 2, 1 - yl)
    core_start(0)
    back(1, -1, yl)
    back(1, 0, 1 - yl)
    items.near(1)
    items.far(0)
    u_cross(0)
    u_out(0)
    g_step(1, 1, 1)
    back(1, 2, yl)
    back(1, 1, 1 - yl)
    back(1, -1, 1 - yl)
    g_step(1, 1, 2)
    back(1, 2, 1 - yl)
    core_start(1)
    items.far(1)
    u_cross(1)
    u_out(1)
    u_mid(0)

    def gain_i_wait(k, total):
        remote(gs, gr.at[k], sem_g1s.at[k], sem_g1r.at[k], peer_i(k)).wait()
        return total + gr[k]

    low = lax.broadcasted_iota(jnp.int32, (8, 128), 1) < 64
    top = lax.broadcasted_iota(jnp.int32, (8, 128), 0) < 4
    gt[...] = jnp.where(top, lax.fori_loop(1, 8, gain_i_wait, gs[...]), cats)
    gr2[u] = gt[...]

    def all_to_all(src, dst, ssem, rsem):
        def body(k, _):
            remote(src((u + k) % 32), dst.at[u], ssem.at[0], rsem.at[0], peer_u(k)).start()
            return 0

        lax.fori_loop(1, 32, body, 0)

    def all_arrived(dst, ssem, rsem):
        every = dst.at[pl.ds(0, 31)]
        remote(every, every, ssem.at[0], rsem.at[0], core).wait()

    all_to_all(lambda t: gt, gr2, sem_g2s, sem_g2r)
    u_mid(1)
    for d in range(-3, 5):
        items.settle(d)
    mine = jnp.concatenate(
        [
            jnp.concatenate([value[:, 0:8], value[:, 8:16]], axis=0)
            for value in (u_final(0), u_final(1))
        ],
        axis=1,
    ).astype(BF16)
    for zs in range(8):
        for half in range(2):
            sumb[zs * 2 + half] = mine[zs, :, half * 128 : half * 128 + 128]

    st[u] = sumb[u // 2]

    all_to_all(lambda t: sumb.at[t // 2], st, sem_1s, sem_1r)
    all_arrived(gr2, sem_g2s, sem_g2r)
    for p in range(16):
        even = jnp.broadcast_to(gr2[p * 2, 4:5, :], (8, 128))
        odd = jnp.broadcast_to(gr2[p * 2 + 1, 4:5, :], (8, 128))
        catl[p] = jnp.where(low, even, odd)

    for p in range(16):
        cat16 = jnp.concatenate([catl[p], catl[p]], axis=0)
        value = sumb[p].astype(F32)
        for expert in range(4):
            ms[expert * 16 : expert * 16 + 16, p * 128 : p * 128 + 128] = jnp.where(
                cat16 == float(expert), value, 0.0
            ).astype(BF16)
    grads = jnp.zeros((64, 512), F32)
    for zs in range(8):
        grads = grads + jnp.dot(
            ms[:, zs * 256 : zs * 256 + 256], xg[zs].reshape(256, 512), preferred_element_type=F32
        )
    wide = jnp.transpose(jnp.concatenate([grads, grads], axis=0)).reshape(32, 2, 8, 128)
    es[...] = jnp.where(low[None], wide[:, 0], wide[:, 1])
    er[u] = es[u]

    all_to_all(lambda t: es.at[t], er, sem_2s, sem_2r)
    gr[0] = jnp.sum(gr2[...], axis=0)
    grow = gr[0, pl.ds(j // 2, 1), :]
    gg_out[...] = jnp.where(j % 2 == 0, grow[:, 0:64], grow[:, 64:128])

    for copy in sent:
        copy.wait_send()
    all_arrived(st, sem_1s, sem_1r)
    wide = st[...].astype(F32)
    sums = jnp.concatenate([wide[:, 0:8], wide[:, 8:16]], axis=0).reshape(512, 128)
    cat1 = catl[u // 2][0:1, :]
    total = jnp.zeros((512, 128), F32)
    for expert in range(4):
        masked = jnp.where(cat1 == float(expert), sums, 0.0).astype(BF16)
        total = total + jnp.dot(w[expert], masked, preferred_element_type=F32)
    igt[...] = jnp.transpose(total)
    ig_out[...] = igt[pl.ds(pl.multiple_of(c * 64, 64), 64), :].astype(BF16)

    all_arrived(er, sem_2s, sem_2r)
    lane = lax.broadcasted_iota(jnp.int32, (8, 128), 1) // 8
    for expert in range(4):
        for half in range(2):
            for t in range(4):
                line = jnp.zeros((8, 128), F32)
                for k in range(16):
                    shift = k * 8 - half * 64 - expert * 16 - (t // 2) * 8
                    moved = pltpu.roll(er[(t % 2) * 16 + k], shift % 128, 1)
                    line = jnp.where(lane == k, moved, line)
                eg_out[expert, half * 8 : half * 8 + 8, t * 128 : t * 128 + 128] = line


def settle(ug, ig, eg, gg, ug_out, ig_out, eg_out, gg_out):
    for src, dst in ((ug, ug_out), (ig, ig_out), (eg, eg_out), (gg, gg_out)):
        dst[...] = src[...]


def on_device(
    user_feat, cotangent, gain, item_feat, categories, expert_w, tile_place, tile_level, tile_count
):
    vmem = pl.BlockSpec(memory_space=pltpu.VMEM)
    smem = pl.BlockSpec(memory_space=pltpu.SMEM)
    hbm = pl.BlockSpec(memory_space=pl.ANY)
    V = pltpu.VMEM
    scratch = [
        V((8, 4, 64, 512), BF16), V((2, 8, 4, 64, 256), BF16), V((4, 512, 512), BF16), V((80, 128, 128), jnp.int32),
        V((2048, 2048), BF16), V((2, 16, 128, 256), F32),
        V((256, 512), BF16), V((256, 512), BF16), V((16, 8, 128), F32),
        V((8, 128), jnp.int32), pltpu.SMEM((8, 128), jnp.int32),
        V((2, 2, 2, 2, 2, 128, 256), BF16), V((2, 2, 2, 2, 2, 128, 256), BF16),
        V((5, 2, 128, 256), BF16), V((5, 2, 128, 256), BF16),
        V((2, 8, 2, 128, 256), BF16), V((256, 256), BF16), V((2, 8, 256, 256), F32),
        V((2, 8, 2, 4, 16, 256), BF16), V((2, 8, 2, 4, 16, 256), BF16),
        V((2, 2, 2, 4, 4, 16, 256), BF16), V((2, 2, 2, 4, 4, 16, 256), BF16),
        V((2, 4, 16, 256), BF16), V((2, 4, 16, 256), BF16),
        V((16, 16, 128), BF16), V((32, 16, 128), BF16), V((64, 2048), BF16),
        V((32, 8, 128), F32), V((32, 8, 128), F32), V((128, 512), F32),
        V((8, 128), F32), V((8, 8, 128), F32), V((8, 128), F32), V((32, 8, 128), F32),
        DMA((5,)), DMA((2, 2, 33)), DMA((2, 33)),
        DMA((2, 2, 2, 2, 2)), DMA((2, 2, 2, 2, 2)), DMA((5, 2)), DMA((5, 2)),
        DMA((2, 2, 2, 2, 2)), DMA((2, 2, 2, 2, 2)), DMA((2, 2)), DMA((2, 2)),
        DMA((2, 8)), DMA((2, 8)), DMA((2, 2, 2, 4)), DMA((2, 2, 2, 4)), DMA((2,)), DMA((2,)),
        DMA((1,)), DMA((1,)), DMA((1,)), DMA((1,)), DMA((8,)), DMA((8,)), DMA((1,)), DMA((1,)),
    ]
    shapes = (
        jax.ShapeDtypeStruct((64, 2048), BF16),
        jax.ShapeDtypeStruct((64, 512), BF16),
        jax.ShapeDtypeStruct((4, 16, 512), F32),
        jax.ShapeDtypeStruct((1, 64), F32),
    )
    parts = pl.pallas_call(
        layer,
        out_shape=shapes,
        in_specs=[vmem, vmem, vmem, smem, smem, hbm, hbm, hbm, hbm],
        out_specs=(vmem, vmem, vmem, vmem),
        scratch_shapes=scratch,
        compiler_params=pltpu.CompilerParams(
            collective_id=0, has_side_effects=True, vmem_limit_bytes=60 * 2**20
        ),
    )(
        item_feat[0], categories, gain[None, :], tile_place[0, 0], tile_count, expert_w, tile_level[0, 0],
        user_feat, cotangent,
    )
    ug, ig, eg, gg = pl.pallas_call(
        settle,
        out_shape=shapes,
        in_specs=[vmem] * 4,
        out_specs=(vmem,) * 4,
    )(*parts)
    return ug.T, ig[None], eg, gg[0]


def solution(mesh):
    placed = (
        P("user", None),
        P("user", None),
        P(),
        P("item", "user", None),
        P("item", "user"),
        P("item", None, None),
        P("user", "item", None),
        P("user", "item", None, None, None),
        P("user", "item"),
    )
    return jax.shard_map(
        on_device,
        mesh=mesh,
        in_specs=placed,
        out_specs=(P("user", "item"), P("item", "user", None), P("item", "user", None), P("item")),
        check_vma=False,
    )
```

```python
import jax
import jax.numpy as jnp
from jax import lax
from jax.experimental import pallas as pl
from jax.experimental.pallas import tpu as pltpu
from jax.sharding import PartitionSpec as P

MESH = pl.DeviceIdType.MESH
F32 = jnp.float32
BF16 = jnp.bfloat16
DMA = pltpu.SemaphoreType.DMA
R, L = 0, 1
DIR = (1, -1)


def layer(
    x_ref, cat_ref, gain_ref, place_ref, count_ref, w_hbm, lvl_hbm, uf_hbm, ct_hbm,
    ug_out, ig_out, eg_out, gg_out,
    xg, qg, w, lvl, amat, acc, uf, ct, catl, tab, tabs,
    mxs, mxr, mys, myr, ugall, ugt, acc2,
    cs, cr, rs, rr, ys, yr, sumb, st, ms, es, er, igt, gs, gr, gt, gr2,
    sem_loc, sem_q, sem_f,
    sem_ixs, sem_ixr, sem_iys, sem_iyr, sem_gxs, sem_gxr, sem_gys, sem_gyr,
    sem_ucs, sem_ucr, sem_uzs, sem_uzr, sem_uys, sem_uyr,
    sem_1s, sem_1r, sem_2s, sem_2r, sem_g1s, sem_g1r, sem_g2s, sem_g2r,
):
    u = lax.axis_index("user")
    j = lax.axis_index("item")
    z, yh, c = u // 4, (u // 2) % 2, u % 2
    yl, x = j // 4, j % 4

    def at_z(d):
        return (((z + d + 8) % 8) * 4 + yh * 2 + c, j)

    def at_x(d):
        return (u, yl * 4 + (x + d + 4) % 4)

    def at_zy(d):
        return (((z + d + 8) % 8) * 4 + (1 - yh) * 2 + c, j)

    y_user = (z * 4 + (1 - yh) * 2 + c, j)
    core = (z * 4 + yh * 2 + 1 - c, j)
    y_item = (u, (1 - yl) * 4 + x)

    def peer_u(k):
        return ((u + k) % 32, j)

    def peer_i(k):
        return (u, ((yl + k // 4) % 2) * 4 + (x + k % 4) % 4)

    sent = []

    def remote(src, dst, ssem, rsem, dev):
        return pltpu.make_async_remote_copy(
            src_ref=src, dst_ref=dst, send_sem=ssem, recv_sem=rsem, device_id=dev, device_id_type=MESH
        )

    def send(src, dst, ssem, rsem, dev):
        copy = remote(src, dst, ssem, rsem, dev)
        copy.start()
        sent.append(copy)

    def recv(dst, ssem, rsem, dev):
        remote(dst, dst, ssem, rsem, dev).wait_recv()

    barrier = pltpu.get_barrier_semaphore()
    near_devices = [at_z(1), at_z(-1), at_z(2), at_z(-2)]
    near_devices += [at_x(1), at_x(-1), y_user, y_item, core]
    for dev in near_devices:
        pl.semaphore_signal(barrier, inc=1, device_id=dev, device_id_type=MESH)

    rows = pl.ds(pl.multiple_of(j * 256, 256), 256)
    local = [
        pltpu.make_async_copy(w_hbm, w, sem_loc.at[1]),
        pltpu.make_async_copy(lvl_hbm, lvl, sem_loc.at[0]),
        pltpu.make_async_copy(uf_hbm.at[rows], uf, sem_loc.at[2]),
        pltpu.make_async_copy(ct_hbm.at[rows], ct, sem_loc.at[3]),
    ]
    for copy in local:
        copy.start()

    spot = lax.broadcasted_iota(jnp.int32, (8, 128), 0) * 128 + lax.broadcasted_iota(jnp.int32, (8, 128), 1)

    def place_slot(s, table):
        key = jnp.where(s < count_ref[0, 0], place_ref[s], -1)
        return jnp.where(spot == key, s, table)

    tab[...] = lax.fori_loop(0, 80, place_slot, jnp.full((8, 128), -1, jnp.int32))
    table_copy = pltpu.make_async_copy(tab, tabs, sem_loc.at[4])
    table_copy.start()

    cats = (cat_ref[...] - j * 4).astype(F32)
    cats = jnp.broadcast_to(jnp.concatenate([cats, cats], axis=1), (8, 128))
    col = jnp.transpose(cats)[0:64, 0:1]
    feats = x_ref[...].astype(F32)
    xg[z, yh * 2 + c] = x_ref[...]
    local[0].wait()
    total = jnp.zeros((64, 512), F32)
    for expert in range(4):
        masked = jnp.where(col == float(expert), feats, 0.0).astype(BF16)
        total = total + jnp.dot(masked, w[expert], preferred_element_type=F32)
    for fh in range(2):
        qg[fh, z, yh * 2 + c] = total[:, fh * 256 : fh * 256 + 256].astype(BF16)

    def hops(d, k):
        return 4 if (k == 0) == (d == R) else 3

    class Gather:
        def __init__(self, buf, sems, late=False):
            self.buf, self.sems, self.late = buf, sems, late

        def hops(self, d, k):
            return hops(d, 0 if self.late else k)

        def block(self, d, k, cc):
            return self.buf.at[(z + d + 8) % 8, (yh if k == 0 else 1 - yh) * 2 + cc]

        def pair(self, n):
            return self.sems.at[0, n], self.sems.at[1, n]

        def put(self, d, k, n, dev):
            block = self.block(d, k, c)
            send(block, block, *self.pair(n), dev)

        def out(self, k):
            for dist in (2, 1):
                for d in (R, L):
                    self.put(0, k, (d * 2 + k) * 4 + dist - 1, at_z(DIR[d] * dist))
            self.put(0, k, 16 + k, core)

        def begin(self):
            self.put(0, 0, 32, y_user)
            self.out(0)

        def cross(self):
            recv(self.block(0, 1, c), *self.pair(32), y_user)
            if self.late:
                self.put(0, 1, 17, core)
            else:
                self.out(1)

        def take(self, k, dist):
            for d in (R, L):
                if dist > self.hops(d, k):
                    continue
                off, n = -DIR[d] * dist, (d * 2 + k) * 4
                recv(self.block(off, k, c), *self.pair(n + dist - 1), at_z(off))
                if dist == 2 and not (self.late and k == 1):
                    if self.hops(d, k) == 4:
                        self.put(off, k, n + 3, at_z(2 * DIR[d]))
                    self.put(off, k, n + 2, at_z(DIR[d]))
                if self.late and k == 0:
                    self.put(off, 0, (d * 2 + 1) * 4 + dist - 1, y_user)
                self.put(off, k, 16 + (off % 8) * 2 + k, core)

        def near(self, k):
            self.take(k, 2)
            self.take(k, 1)

        def far(self, k):
            self.take(k, 3)
            self.take(k, 4)

        def settle(self, d):
            for k in range(2):
                recv(self.block(d, k, 1 - c), *self.pair(16 + (d % 8) * 2 + k), core)

    queries = [Gather(qg.at[fh], sem_q.at[fh], fh == 1) for fh in range(2)]
    items = Gather(xg, sem_f)

    def build(zs):
        def body(rb, _):
            for half in range(2):
                pos = rb * 16 + zs * 2 + half
                slot = tabs[pos // 128, pos % 128]
                scale = jnp.where(slot >= 0, 1.0 / 256, 0.0)
                tile = lvl[jnp.maximum(slot, 0)].astype(F32) * scale
                col0 = zs * 256 + half * 128
                amat[pl.ds(pl.multiple_of(rb * 128, 128), 128), col0 : col0 + 128] = tile.astype(BF16)
            return 0

        lax.fori_loop(0, 16, body, 0)

    def ihops(d, h):
        return 2 if (h == 0) == (d == R) else 1

    def jat(dx, y):
        return y * 4 + (x + dx + 4) % 4

    def ysel(k):
        return 1 - yl if k == 0 else yl

    def product(fh, dx, k):
        jt = jat(dx, ysel(k))
        part = jnp.dot(
            amat[pl.ds(pl.multiple_of(jt * 256, 256), 256), :],
            qg[fh].reshape(2048, 256),
            preferred_element_type=F32,
        )
        acc[fh, pl.ds(jt * 2, 2)] = part.reshape(2, 128, 256)

    def term(fh, dx, k, h):
        return acc[fh, jat(dx, ysel(k)) * 2 + h]

    def mx_send(fh, d, k, h, s, value):
        n = (fh, d, k, h, s)
        mxs[n] = value.astype(BF16)
        send(mxs.at[n], mxr.at[n], sem_ixs.at[n], sem_ixr.at[n], at_x(DIR[d]))

    def mx_recv(fh, d, k, h, s):
        n = (fh, d, k, h, s)
        recv(mxr.at[n], sem_ixs.at[n], sem_ixr.at[n], at_x(-DIR[d]))
        return mxr[n].astype(F32)

    combos = [(d, h) for d in (R, L) for h in range(2)]

    def far(fh, k):
        for d, h in combos:
            if ihops(d, h) == 2:
                mx_send(fh, d, k, h, 1, term(fh, 2, k, h))

    def near(fh, k):
        for d, h in combos:
            if ihops(d, h) == 1:
                mx_send(fh, d, k, h, 0, term(fh, DIR[d], k, h))

    def relay(fh, k):
        for d, h in combos:
            if ihops(d, h) == 2:
                mx_send(fh, d, k, h, 0, term(fh, DIR[d], k, h) + mx_recv(fh, d, k, h, 1))

    def pair_put(slot, h, value):
        n = (slot, h)
        mys[n] = value.astype(BF16)
        send(mys.at[n], myr.at[n], sem_iys.at[n], sem_iyr.at[n], y_item)

    def pair_take(slot, h):
        n = (slot, h)
        recv(myr.at[n], sem_iys.at[n], sem_iyr.at[n], y_item)
        return myr[n].astype(F32)

    PAIR = {2: 1, 1: 2, -1: 3, 0: 4}

    def pair_last():
        for h in range(2):
            pair_put(0, h, term(0, 0, 0, h) + mx_recv(0, R, 0, h, 0) + mx_recv(0, L, 0, h, 0))

    def pair_first(dx):
        product(1, dx, 0)
        for h in range(2):
            pair_put(PAIR[dx], h, term(1, dx, 0, h))

    def pair_add(dx):
        for h in range(2):
            n = jat(dx, yl) * 2 + h
            acc[1, n] = acc[1, n] + pair_take(PAIR[dx], h)

    def summed(fh, h):
        value = term(fh, 0, 1, h) + mx_recv(fh, R, 1, h, 0) + mx_recv(fh, L, 1, h, 0)
        return value + pair_take(0, h) if fh == 0 else value

    def all_here(fh):
        for d in range(-3, 5):
            queries[fh].settle(d)

    pl.semaphore_wait(barrier, 9)
    queries[0].begin()
    queries[1].begin()
    local[1].wait()
    table_copy.wait()
    for zs in range(4):
        build(zs)
    queries[0].cross()
    queries[0].near(0)
    queries[1].cross()
    queries[1].near(0)
    for zs in range(4, 8):
        build(zs)
    queries[0].near(1)
    queries[0].far(0)
    queries[1].far(0)
    queries[1].near(1)
    queries[0].far(1)
    all_here(0)
    for k in range(2):
        product(0, 2, k)
        far(0, k)
    for k in range(2):
        product(0, 1, k)
        product(0, -1, k)
        near(0, k)
    queries[1].far(1)
    all_here(1)
    for dx in (2, 1, -1, 0):
        pair_first(dx)
    product(0, 0, 0)
    product(0, 0, 1)
    items.begin()
    product(1, 2, 1)
    relay(0, 0)
    relay(0, 1)
    product(1, 1, 1)
    product(1, -1, 1)
    product(1, 0, 1)
    pair_add(2)
    far(1, 1)
    pair_last()
    pair_add(1)
    pair_add(-1)
    near(1, 1)
    relay(1, 1)
    pair_add(0)

    local[2].wait()
    local[3].wait()
    gain = [gain_ref[:, fh * 256 : fh * 256 + 256] for fh in range(2)]
    gsum = [jnp.zeros((1, 256), F32) for fh in range(2)]

    def g_cross_start(fh, h):
        block = ugall.at[fh, j, h]
        send(block, block, sem_gys.at[fh, h], sem_gyr.at[fh, h], y_item)

    def g_ring_start(fh, h, k):
        for d in (R, L):
            block = ugall.at[fh, jat(0, yl if k == 0 else 1 - yl), h]
            send(block, block, sem_gxs.at[fh, d, k, h, 0], sem_gxr.at[fh, d, k, h, 0], at_x(DIR[d]))

    def g_cross(fh):
        for h in range(2):
            recv(ugall.at[fh, jat(0, 1 - yl), h], sem_gys.at[fh, h], sem_gyr.at[fh, h], y_item)
            if fh == 0:
                g_ring_start(fh, h, 1)

    def g_step(fh, k, s):
        y = yl if k == 0 else 1 - yl
        for h in range(2):
            for d in (R, L):
                if s > ihops(d, h):
                    continue
                block = ugall.at[fh, jat(-DIR[d] * s, y), h]
                n = (fh, d, k, h, s - 1)
                recv(block, sem_gxs.at[n], sem_gxr.at[n], at_x(-DIR[d]))
                if s < ihops(d, h) and (fh == 0 or k == 0):
                    n = (fh, d, k, h, s)
                    send(block, block, sem_gxs.at[n], sem_gxr.at[n], at_x(DIR[d]))
                if fh == 1 and k == 0:
                    n = (fh, d, 1, h, s - 1)
                    send(block, block, sem_gxs.at[n], sem_gxr.at[n], y_item)

    for h in range(2):
        feat_rows = slice(h * 128, h * 128 + 128)
        pre, grad = [], []
        for fh in range(2):
            cols = slice(fh * 256, fh * 256 + 256)
            pre.append(uf[feat_rows, cols].astype(F32) + summed(fh, h))
            grad.append(ct[feat_rows, cols].astype(F32))
        squares = sum(jnp.sum(p * p, axis=-1, keepdims=True) for p in pre)
        crossed = sum(jnp.sum(gain[fh] * grad[fh] * pre[fh], axis=-1, keepdims=True) for fh in range(2))
        inv = lax.rsqrt(squares * (1.0 / 512) + 1e-05)
        factor = inv * inv * inv * (crossed * (1.0 / 512))
        for fh in range(2):
            ugall[fh, j, h] = (inv * (gain[fh] * grad[fh]) - factor * pre[fh]).astype(BF16)
            gsum[fh] = gsum[fh] + jnp.sum(grad[fh] * pre[fh] * inv, axis=0, keepdims=True)
        g_cross_start(0, h)
        g_ring_start(0, h, 0)
    for h in range(2):
        g_cross_start(1, h)
        g_ring_start(1, h, 0)
    gs[...] = jnp.zeros((8, 128), F32)
    for t in range(4):
        gs[t : t + 1, :] = gsum[t // 2][:, (t % 2) * 128 : (t % 2) * 128 + 128]

    def gain_i(k, _):
        remote(gs, gr.at[k], sem_g1s.at[k], sem_g1r.at[k], peer_i(k)).start()
        return 0

    lax.fori_loop(1, 8, gain_i, 0)

    def back(fh, dx, y, first=False):
        jj = jat(dx, y)
        ugt[...] = jnp.transpose(ugall[fh, jj].reshape(256, 256).astype(F32)).astype(BF16)
        for zs in range(8):
            part = jnp.dot(
                ugt[...],
                amat[pl.ds(pl.multiple_of(jj * 256, 256), 256), zs * 256 : zs * 256 + 256],
                preferred_element_type=F32,
            )
            acc2[fh, zs] = part if first else acc2[fh, zs] + part

        @pl.when(j // 4 == fh)
        def _():
            ug_out[:, pl.ds(pl.multiple_of(jj * 256, 256), 256)] = ugt[
                pl.ds(pl.multiple_of((j % 4) * 64, 64), 64), :
            ]

    def piece(fh, zs, y, cc):
        v = acc2[fh, :, pl.ds(pl.multiple_of((zs * 4 + y * 2 + cc) * 8, 8), 8), :]
        return jnp.concatenate([v[0:4], v[4:8]], axis=1)

    def core_start(fh):
        for d in (4, 3, -3, 1, -1, 2, -2, 0):
            zs = (z + d + 8) % 8
            for y in range(2):
                cs[fh, zs, y] = piece(fh, zs, y, 1 - c).astype(BF16)
            send(cs.at[fh, zs], cr.at[fh, zs], sem_ucs.at[fh, d % 8], sem_ucr.at[fh, d % 8], core)

    def core_recv(fh, d):
        recv(cr.at[fh, (z + d + 8) % 8], sem_ucs.at[fh, d % 8], sem_ucr.at[fh, d % 8], core)

    def own_sum(fh, d, y):
        zs = (z + d + 8) % 8
        return piece(fh, zs, y, c) + cr[fh, zs, y].astype(F32)

    def z_send(fh, d, k, slot, value, dist):
        n = (fh, d, k, slot)
        rs[n] = value.astype(BF16)
        dev = at_zy(DIR[d] * dist) if k == 0 and slot < 2 else at_z(DIR[d] * dist)
        send(rs.at[n], rr.at[n], sem_uzs.at[n], sem_uzr.at[n], dev)

    def z_recv(fh, d, k, slot):
        n = (fh, d, k, slot)
        recv(rr.at[n], sem_uzs.at[n], sem_uzr.at[n], at_z(-DIR[d]))
        return rr[n].astype(F32)

    def uy(k):
        return 1 - yh if k == 0 else yh

    ucombos = [(k, d) for k in range(2) for d in (R, L)]

    def u_out(fh):
        core_recv(fh, 4)
        for k, d in ucombos:
            if hops(d, k) == 4:
                z_send(fh, d, k, 3, own_sum(fh, 4, uy(k)), 2)
        for dist, slot in ((3, 2), (1, 0)):
            core_recv(fh, dist)
            core_recv(fh, -dist)
            for k, d in ucombos:
                z_send(fh, d, k, slot, own_sum(fh, DIR[d] * dist, uy(k)), 1)

    def u_mid(fh):
        core_recv(fh, 2)
        core_recv(fh, -2)
        for k, d in ucombos:
            value = own_sum(fh, DIR[d] * 2, uy(k)) + z_recv(fh, d, k, 2)
            if hops(d, k) == 4:
                value = value + z_recv(fh, d, k, 3)
            z_send(fh, d, k, 1, value, 2)

    def u_cross(fh):
        core_recv(fh, 0)
        ys[fh] = own_sum(fh, 0, 1 - yh).astype(BF16)
        send(ys.at[fh], yr.at[fh], sem_uys.at[fh], sem_uyr.at[fh], y_user)

    def u_final(fh):
        mine = own_sum(fh, 0, yh)
        for k, d in ucombos:
            mine = mine + z_recv(fh, d, k, 0) + z_recv(fh, d, k, 1)
        recv(yr.at[fh], sem_uys.at[fh], sem_uyr.at[fh], y_user)
        return mine + yr[fh].astype(F32)

    def gain_i_wait(k, total):
        remote(gs, gr.at[k], sem_g1s.at[k], sem_g1r.at[k], peer_i(k)).wait()
        return total + gr[k]

    low = lax.broadcasted_iota(jnp.int32, (8, 128), 1) < 64
    top = lax.broadcasted_iota(jnp.int32, (8, 128), 0) < 4
    def all_to_all(src, dst, ssem, rsem):
        def body(k, _):
            remote(src((u + k) % 32), dst.at[u], ssem.at[0], rsem.at[0], peer_u(k)).start()
            return 0

        lax.fori_loop(1, 32, body, 0)

    def all_arrived(dst, ssem, rsem):
        every = dst.at[pl.ds(0, 31)]
        remote(every, every, ssem.at[0], rsem.at[0], core).wait()

    back(0, 0, yl, True)
    items.cross()
    back(1, 0, yl, True)
    g_cross(0)
    g_step(0, 0, 1)
    g_step(1, 0, 1)
    back(0, 1, yl)
    back(0, -1, yl)
    items.near(0)
    g_cross(1)
    back(0, 0, 1 - yl)
    back(1, 1, yl)
    g_step(0, 1, 1)
    back(0, 1, 1 - yl)
    g_step(0, 0, 2)
    back(0, 2, yl)
    g_step(1, 0, 2)
    back(0, -1, 1 - yl)
    gt[...] = jnp.where(top, lax.fori_loop(1, 8, gain_i_wait, gs[...]), cats)
    gr2[u] = gt[...]

    all_to_all(lambda t: gt, gr2, sem_g2s, sem_g2r)
    g_step(0, 1, 2)
    back(0, 2, 1 - yl)
    core_start(0)
    back(1, -1, yl)
    back(1, 0, 1 - yl)
    items.near(1)
    items.far(0)
    u_out(0)
    u_cross(0)
    g_step(1, 1, 1)
    back(1, 2, yl)
    back(1, 1, 1 - yl)
    back(1, -1, 1 - yl)
    g_step(1, 1, 2)
    back(1, 2, 1 - yl)
    core_start(1)
    items.far(1)
    u_out(1)
    u_cross(1)
    u_mid(0)
    all_arrived(gr2, sem_g2s, sem_g2r)
    for p in range(16):
        even = jnp.broadcast_to(gr2[p * 2, 4:5, :], (8, 128))
        odd = jnp.broadcast_to(gr2[p * 2 + 1, 4:5, :], (8, 128))
        catl[p] = jnp.where(low, even, odd)
    gr[0] = jnp.sum(gr2[...], axis=0)
    grow = gr[0, pl.ds(j // 2, 1), :]
    gg_out[...] = jnp.where(j % 2 == 0, grow[:, 0:64], grow[:, 64:128])
    u_mid(1)
    for d in range(-3, 5):
        items.settle(d)
    mine = jnp.concatenate(
        [
            jnp.concatenate([value[:, 0:8], value[:, 8:16]], axis=0)
            for value in (u_final(0), u_final(1))
        ],
        axis=1,
    ).astype(BF16)
    for zs in range(8):
        for half in range(2):
            sumb[zs * 2 + half] = mine[zs, :, half * 128 : half * 128 + 128]

    st[u] = sumb[u // 2]

    all_to_all(lambda t: sumb.at[t // 2], st, sem_1s, sem_1r)
    for p in range(16):
        cat16 = jnp.concatenate([catl[p], catl[p]], axis=0)
        value = sumb[p].astype(F32)
        for expert in range(4):
            ms[expert * 16 : expert * 16 + 16, p * 128 : p * 128 + 128] = jnp.where(
                cat16 == float(expert), value, 0.0
            ).astype(BF16)
    grads = jnp.zeros((64, 512), F32)
    for zs in range(8):
        grads = grads + jnp.dot(
            ms[:, zs * 256 : zs * 256 + 256], xg[zs].reshape(256, 512), preferred_element_type=F32
        )
    wide = jnp.transpose(jnp.concatenate([grads, grads], axis=0)).reshape(32, 2, 8, 128)
    es[...] = jnp.where(low[None], wide[:, 0], wide[:, 1])
    er[u] = es[u]

    all_to_all(lambda t: es.at[t], er, sem_2s, sem_2r)
    for copy in sent:
        copy.wait_send()
    all_arrived(st, sem_1s, sem_1r)
    wide = st[...].astype(F32)
    sums = jnp.concatenate([wide[:, 0:8], wide[:, 8:16]], axis=0).reshape(512, 128)
    cat1 = catl[u // 2][0:1, :]
    total = jnp.zeros((512, 128), F32)
    for expert in range(4):
        masked = jnp.where(cat1 == float(expert), sums, 0.0).astype(BF16)
        total = total + jnp.dot(w[expert], masked, preferred_element_type=F32)
    igt[...] = jnp.transpose(total)
    ig_out[...] = igt[pl.ds(pl.multiple_of(c * 64, 64), 64), :].astype(BF16)

    all_arrived(er, sem_2s, sem_2r)
    lane = lax.broadcasted_iota(jnp.int32, (8, 128), 1) // 8
    for expert in range(4):
        for half in range(2):
            for t in range(4):
                line = jnp.zeros((8, 128), F32)
                for k in range(16):
                    shift = k * 8 - half * 64 - expert * 16 - (t // 2) * 8
                    moved = pltpu.roll(er[(t % 2) * 16 + k], shift % 128, 1)
                    line = jnp.where(lane == k, moved, line)
                eg_out[expert, half * 8 : half * 8 + 8, t * 128 : t * 128 + 128] = line


def settle(ug, ig, eg, gg, ug_out, ig_out, eg_out, gg_out):
    for src, dst in ((ug, ug_out), (ig, ig_out), (eg, eg_out), (gg, gg_out)):
        dst[...] = src[...]


def on_device(
    user_feat, cotangent, gain, item_feat, categories, expert_w, tile_place, tile_level, tile_count
):
    vmem = pl.BlockSpec(memory_space=pltpu.VMEM)
    smem = pl.BlockSpec(memory_space=pltpu.SMEM)
    hbm = pl.BlockSpec(memory_space=pl.ANY)
    V = pltpu.VMEM
    scratch = [
        V((8, 4, 64, 512), BF16), V((2, 8, 4, 64, 256), BF16), V((4, 512, 512), BF16), V((80, 128, 128), jnp.int32),
        V((2048, 2048), BF16), V((2, 16, 128, 256), F32),
        V((256, 512), BF16), V((256, 512), BF16), V((16, 8, 128), F32),
        V((8, 128), jnp.int32), pltpu.SMEM((8, 128), jnp.int32),
        V((2, 2, 2, 2, 2, 128, 256), BF16), V((2, 2, 2, 2, 2, 128, 256), BF16),
        V((5, 2, 128, 256), BF16), V((5, 2, 128, 256), BF16),
        V((2, 8, 2, 128, 256), BF16), V((256, 256), BF16), V((2, 8, 256, 256), F32),
        V((2, 8, 2, 4, 16, 256), BF16), V((2, 8, 2, 4, 16, 256), BF16),
        V((2, 2, 2, 4, 4, 16, 256), BF16), V((2, 2, 2, 4, 4, 16, 256), BF16),
        V((2, 4, 16, 256), BF16), V((2, 4, 16, 256), BF16),
        V((16, 16, 128), BF16), V((32, 16, 128), BF16), V((64, 2048), BF16),
        V((32, 8, 128), F32), V((32, 8, 128), F32), V((128, 512), F32),
        V((8, 128), F32), V((8, 8, 128), F32), V((8, 128), F32), V((32, 8, 128), F32),
        DMA((5,)), DMA((2, 2, 33)), DMA((2, 33)),
        DMA((2, 2, 2, 2, 2)), DMA((2, 2, 2, 2, 2)), DMA((5, 2)), DMA((5, 2)),
        DMA((2, 2, 2, 2, 2)), DMA((2, 2, 2, 2, 2)), DMA((2, 2)), DMA((2, 2)),
        DMA((2, 8)), DMA((2, 8)), DMA((2, 2, 2, 4)), DMA((2, 2, 2, 4)), DMA((2,)), DMA((2,)),
        DMA((1,)), DMA((1,)), DMA((1,)), DMA((1,)), DMA((8,)), DMA((8,)), DMA((1,)), DMA((1,)),
    ]
    shapes = (
        jax.ShapeDtypeStruct((64, 2048), BF16),
        jax.ShapeDtypeStruct((64, 512), BF16),
        jax.ShapeDtypeStruct((4, 16, 512), F32),
        jax.ShapeDtypeStruct((1, 64), F32),
    )
    parts = pl.pallas_call(
        layer,
        out_shape=shapes,
        in_specs=[vmem, vmem, vmem, smem, smem, hbm, hbm, hbm, hbm],
        out_specs=(vmem, vmem, vmem, vmem),
        scratch_shapes=scratch,
        compiler_params=pltpu.CompilerParams(
            collective_id=0, has_side_effects=True, vmem_limit_bytes=60 * 2**20
        ),
    )(
        item_feat[0], categories, gain[None, :], tile_place[0, 0], tile_count, expert_w, tile_level[0, 0],
        user_feat, cotangent,
    )
    ug, ig, eg, gg = pl.pallas_call(
        settle,
        out_shape=shapes,
        in_specs=[vmem] * 4,
        out_specs=(vmem,) * 4,
    )(*parts)
    return ug.T, ig[None], eg, gg[0]


def solution(mesh):
    placed = (
        P("user", None),
        P("user", None),
        P(),
        P("item", "user", None),
        P("item", "user"),
        P("item", None, None),
        P("user", "item", None),
        P("user", "item", None, None, None),
        P("user", "item"),
    )
    return jax.shard_map(
        on_device,
        mesh=mesh,
        in_specs=placed,
        out_specs=(P("user", "item"), P("item", "user", None), P("item", "user", None), P("item")),
        check_vma=False,
    )
```

```python
import jax
import jax.numpy as jnp
from jax import lax
from jax.experimental import pallas as pl
from jax.experimental.pallas import tpu as pltpu
from jax.sharding import PartitionSpec as P

MESH = pl.DeviceIdType.MESH
F32 = jnp.float32
BF16 = jnp.bfloat16
DMA = pltpu.SemaphoreType.DMA
R, L = 0, 1
DIR = (1, -1)


def layer(
    x_ref, cat_ref, gain_ref, place_ref, count_ref, w_hbm, lvl_hbm, uf_hbm, ct_hbm,
    ug_out, ig_out, eg_out, gg_out,
    xg, qg, w, lvl, amat, acc, uf, ct, catl, tab, tabs,
    mxs, mxr, mys, myr, ugall, ugt, acc2,
    cs, cr, rs, rr, ys, yr, sumb, st, ms, es, er, igt, gs, gr, gt, gr2,
    sem_loc, sem_q, sem_f,
    sem_ixs, sem_ixr, sem_iys, sem_iyr, sem_gxs, sem_gxr, sem_gys, sem_gyr,
    sem_ucs, sem_ucr, sem_uzs, sem_uzr, sem_uys, sem_uyr,
    sem_1s, sem_1r, sem_2s, sem_2r, sem_g1s, sem_g1r, sem_g2s, sem_g2r,
):
    u = lax.axis_index("user")
    j = lax.axis_index("item")
    z, yh, c = u // 4, (u // 2) % 2, u % 2
    yl, x = j // 4, j % 4

    def at_z(d):
        return (((z + d + 8) % 8) * 4 + yh * 2 + c, j)

    def at_x(d):
        return (u, yl * 4 + (x + d + 4) % 4)

    def at_zy(d):
        return (((z + d + 8) % 8) * 4 + (1 - yh) * 2 + c, j)

    y_user = (z * 4 + (1 - yh) * 2 + c, j)
    core = (z * 4 + yh * 2 + 1 - c, j)
    y_item = (u, (1 - yl) * 4 + x)

    def peer_u(k):
        return ((u + k) % 32, j)

    def peer_i(k):
        return (u, ((yl + k // 4) % 2) * 4 + (x + k % 4) % 4)

    sent = []

    def remote(src, dst, ssem, rsem, dev):
        return pltpu.make_async_remote_copy(
            src_ref=src, dst_ref=dst, send_sem=ssem, recv_sem=rsem, device_id=dev, device_id_type=MESH
        )

    def send(src, dst, ssem, rsem, dev):
        copy = remote(src, dst, ssem, rsem, dev)
        copy.start()
        sent.append(copy)

    def recv(dst, ssem, rsem, dev):
        remote(dst, dst, ssem, rsem, dev).wait_recv()

    barrier = pltpu.get_barrier_semaphore()
    near_devices = [at_z(1), at_z(-1), at_z(2), at_z(-2)]
    near_devices += [at_x(1), at_x(-1), y_user, y_item, core]
    for dev in near_devices:
        pl.semaphore_signal(barrier, inc=1, device_id=dev, device_id_type=MESH)

    rows = pl.ds(pl.multiple_of(j * 256, 256), 256)
    local = [
        pltpu.make_async_copy(w_hbm, w, sem_loc.at[1]),
        pltpu.make_async_copy(lvl_hbm, lvl, sem_loc.at[0]),
        pltpu.make_async_copy(uf_hbm.at[rows], uf, sem_loc.at[2]),
        pltpu.make_async_copy(ct_hbm.at[rows], ct, sem_loc.at[3]),
    ]
    for copy in local:
        copy.start()

    spot = lax.broadcasted_iota(jnp.int32, (8, 128), 0) * 128 + lax.broadcasted_iota(jnp.int32, (8, 128), 1)

    def place_slot(s, table):
        key = jnp.where(s < count_ref[0, 0], place_ref[s], -1)
        return jnp.where(spot == key, s, table)

    tab[...] = lax.fori_loop(0, 80, place_slot, jnp.full((8, 128), -1, jnp.int32))
    table_copy = pltpu.make_async_copy(tab, tabs, sem_loc.at[4])
    table_copy.start()

    cats = (cat_ref[...] - j * 4).astype(F32)
    cats = jnp.broadcast_to(jnp.concatenate([cats, cats], axis=1), (8, 128))
    col = jnp.transpose(cats)[0:64, 0:1]
    feats = x_ref[...].astype(F32)
    xg[z, yh * 2 + c] = x_ref[...]
    local[0].wait()
    total = jnp.zeros((64, 512), F32)
    for expert in range(4):
        masked = jnp.where(col == float(expert), feats, 0.0).astype(BF16)
        total = total + jnp.dot(masked, w[expert], preferred_element_type=F32)
    for fh in range(2):
        qg[fh, z, yh * 2 + c] = total[:, fh * 256 : fh * 256 + 256].astype(BF16)

    def hops(d, k):
        return 4 if (k == 0) == (d == R) else 3

    class Gather:
        def __init__(self, buf, sems, late=False):
            self.buf, self.sems, self.late = buf, sems, late

        def hops(self, d, k):
            return hops(d, 0 if self.late else k)

        def block(self, d, k, cc):
            return self.buf.at[(z + d + 8) % 8, (yh if k == 0 else 1 - yh) * 2 + cc]

        def pair(self, n):
            return self.sems.at[0, n], self.sems.at[1, n]

        def put(self, d, k, n, dev):
            block = self.block(d, k, c)
            send(block, block, *self.pair(n), dev)

        def out(self, k):
            for dist in (2, 1):
                for d in (R, L):
                    self.put(0, k, (d * 2 + k) * 4 + dist - 1, at_z(DIR[d] * dist))
            self.put(0, k, 16 + k, core)

        def begin(self):
            self.put(0, 0, 32, y_user)
            self.out(0)

        def cross(self):
            recv(self.block(0, 1, c), *self.pair(32), y_user)
            if self.late:
                self.put(0, 1, 17, core)
            else:
                self.out(1)

        def take(self, k, dist):
            for d in (R, L):
                if dist > self.hops(d, k):
                    continue
                off, n = -DIR[d] * dist, (d * 2 + k) * 4
                recv(self.block(off, k, c), *self.pair(n + dist - 1), at_z(off))
                if dist == 2 and not (self.late and k == 1):
                    if self.hops(d, k) == 4:
                        self.put(off, k, n + 3, at_z(2 * DIR[d]))
                    self.put(off, k, n + 2, at_z(DIR[d]))
                if self.late and k == 0:
                    self.put(off, 0, (d * 2 + 1) * 4 + dist - 1, y_user)
                self.put(off, k, 16 + (off % 8) * 2 + k, core)

        def near(self, k):
            self.take(k, 2)
            self.take(k, 1)

        def far(self, k):
            self.take(k, 3)
            self.take(k, 4)

        def settle(self, d):
            for k in range(2):
                recv(self.block(d, k, 1 - c), *self.pair(16 + (d % 8) * 2 + k), core)

    queries = [Gather(qg.at[fh], sem_q.at[fh], fh == 1) for fh in range(2)]
    items = Gather(xg, sem_f)

    def build(zs):
        def body(rb, _):
            for half in range(2):
                pos = rb * 16 + zs * 2 + half
                slot = tabs[pos // 128, pos % 128]
                scale = jnp.where(slot >= 0, 1.0 / 256, 0.0)
                tile = lvl[jnp.maximum(slot, 0)].astype(F32) * scale
                col0 = zs * 256 + half * 128
                amat[pl.ds(pl.multiple_of(rb * 128, 128), 128), col0 : col0 + 128] = tile.astype(BF16)
            return 0

        lax.fori_loop(0, 16, body, 0)

    def ihops(d, h):
        return 2 if (h == 0) == (d == R) else 1

    def jat(dx, y):
        return y * 4 + (x + dx + 4) % 4

    def ysel(k):
        return 1 - yl if k == 0 else yl

    def product(fh, dx, k):
        jt = jat(dx, ysel(k))
        part = jnp.dot(
            amat[pl.ds(pl.multiple_of(jt * 256, 256), 256), :],
            qg[fh].reshape(2048, 256),
            preferred_element_type=F32,
        )
        acc[fh, pl.ds(jt * 2, 2)] = part.reshape(2, 128, 256)

    def term(fh, dx, k, h):
        return acc[fh, jat(dx, ysel(k)) * 2 + h]

    def mx_send(fh, d, k, h, s, value):
        n = (fh, d, k, h, s)
        mxs[n] = value.astype(BF16)
        send(mxs.at[n], mxr.at[n], sem_ixs.at[n], sem_ixr.at[n], at_x(DIR[d]))

    def mx_recv(fh, d, k, h, s):
        n = (fh, d, k, h, s)
        recv(mxr.at[n], sem_ixs.at[n], sem_ixr.at[n], at_x(-DIR[d]))
        return mxr[n].astype(F32)

    combos = [(d, h) for d in (R, L) for h in range(2)]

    def far(fh, k):
        for d, h in combos:
            if ihops(d, h) == 2:
                mx_send(fh, d, k, h, 1, term(fh, 2, k, h))

    def near(fh, k):
        for d, h in combos:
            if ihops(d, h) == 1:
                mx_send(fh, d, k, h, 0, term(fh, DIR[d], k, h))

    def relay(fh, k):
        for d, h in combos:
            if ihops(d, h) == 2:
                mx_send(fh, d, k, h, 0, term(fh, DIR[d], k, h) + mx_recv(fh, d, k, h, 1))

    def pair_put(slot, h, value):
        n = (slot, h)
        mys[n] = value.astype(BF16)
        send(mys.at[n], myr.at[n], sem_iys.at[n], sem_iyr.at[n], y_item)

    def pair_take(slot, h):
        n = (slot, h)
        recv(myr.at[n], sem_iys.at[n], sem_iyr.at[n], y_item)
        return myr[n].astype(F32)

    PAIR = {2: 1, 1: 2, -1: 3, 0: 4}

    def pair_last():
        for h in range(2):
            pair_put(0, h, term(0, 0, 0, h) + mx_recv(0, R, 0, h, 0) + mx_recv(0, L, 0, h, 0))

    def pair_first(dx):
        product(1, dx, 0)
        for h in range(2):
            pair_put(PAIR[dx], h, term(1, dx, 0, h))

    def pair_add(dx):
        for h in range(2):
            n = jat(dx, yl) * 2 + h
            acc[1, n] = acc[1, n] + pair_take(PAIR[dx], h)

    def summed(fh, h):
        value = term(fh, 0, 1, h) + mx_recv(fh, R, 1, h, 0) + mx_recv(fh, L, 1, h, 0)
        return value + pair_take(0, h) if fh == 0 else value

    def all_here(fh):
        for d in range(-3, 5):
            queries[fh].settle(d)

    pl.semaphore_wait(barrier, 9)
    queries[0].begin()
    queries[1].begin()
    local[1].wait()
    table_copy.wait()
    for zs in range(4):
        build(zs)
    queries[0].cross()
    queries[0].near(0)
    queries[1].cross()
    queries[1].near(0)
    for zs in range(4, 8):
        build(zs)
    queries[0].near(1)
    queries[0].far(0)
    queries[1].far(0)
    queries[1].near(1)
    queries[0].far(1)
    all_here(0)
    for k in range(2):
        product(0, 2, k)
        far(0, k)
    for k in range(2):
        product(0, 1, k)
        product(0, -1, k)
        near(0, k)
    queries[1].far(1)
    all_here(1)
    for dx in (2, 1, -1, 0):
        pair_first(dx)
    product(0, 0, 0)
    product(0, 0, 1)
    items.begin()
    product(1, 2, 1)
    relay(0, 0)
    relay(0, 1)
    product(1, 1, 1)
    product(1, -1, 1)
    product(1, 0, 1)
    pair_add(2)
    far(1, 1)
    pair_last()
    pair_add(1)
    pair_add(-1)
    near(1, 1)
    relay(1, 1)
    pair_add(0)

    local[2].wait()
    local[3].wait()
    gain = [gain_ref[:, fh * 256 : fh * 256 + 256] for fh in range(2)]
    gsum = [jnp.zeros((1, 256), F32) for fh in range(2)]

    def g_cross_start(fh, h):
        block = ugall.at[fh, j, h]
        send(block, block, sem_gys.at[fh, h], sem_gyr.at[fh, h], y_item)

    def g_ring_start(fh, h, k):
        for d in (R, L):
            block = ugall.at[fh, jat(0, yl if k == 0 else 1 - yl), h]
            send(block, block, sem_gxs.at[fh, d, k, h, 0], sem_gxr.at[fh, d, k, h, 0], at_x(DIR[d]))

    def g_cross(fh):
        for h in range(2):
            recv(ugall.at[fh, jat(0, 1 - yl), h], sem_gys.at[fh, h], sem_gyr.at[fh, h], y_item)
            if fh == 0:
                g_ring_start(fh, h, 1)

    def g_step(fh, k, s):
        y = yl if k == 0 else 1 - yl
        for h in range(2):
            for d in (R, L):
                if s > ihops(d, h):
                    continue
                block = ugall.at[fh, jat(-DIR[d] * s, y), h]
                n = (fh, d, k, h, s - 1)
                recv(block, sem_gxs.at[n], sem_gxr.at[n], at_x(-DIR[d]))
                if s < ihops(d, h) and (fh == 0 or k == 0):
                    n = (fh, d, k, h, s)
                    send(block, block, sem_gxs.at[n], sem_gxr.at[n], at_x(DIR[d]))
                if fh == 1 and k == 0:
                    n = (fh, d, 1, h, s - 1)
                    send(block, block, sem_gxs.at[n], sem_gxr.at[n], y_item)

    for h in range(2):
        feat_rows = slice(h * 128, h * 128 + 128)
        pre, grad = [], []
        for fh in range(2):
            cols = slice(fh * 256, fh * 256 + 256)
            pre.append(uf[feat_rows, cols].astype(F32) + summed(fh, h))
            grad.append(ct[feat_rows, cols].astype(F32))
        squares = sum(jnp.sum(p * p, axis=-1, keepdims=True) for p in pre)
        crossed = sum(jnp.sum(gain[fh] * grad[fh] * pre[fh], axis=-1, keepdims=True) for fh in range(2))
        inv = lax.rsqrt(squares * (1.0 / 512) + 1e-05)
        factor = inv * inv * inv * (crossed * (1.0 / 512))
        for fh in range(2):
            ugall[fh, j, h] = (inv * (gain[fh] * grad[fh]) - factor * pre[fh]).astype(BF16)
            gsum[fh] = gsum[fh] + jnp.sum(grad[fh] * pre[fh] * inv, axis=0, keepdims=True)
        g_cross_start(0, h)
        g_ring_start(0, h, 0)
    for h in range(2):
        g_cross_start(1, h)
        g_ring_start(1, h, 0)
    gs[...] = jnp.zeros((8, 128), F32)
    for t in range(4):
        gs[t : t + 1, :] = gsum[t // 2][:, (t % 2) * 128 : (t % 2) * 128 + 128]

    def gain_i(k, _):
        remote(gs, gr.at[k], sem_g1s.at[k], sem_g1r.at[k], peer_i(k)).start()
        return 0

    lax.fori_loop(1, 8, gain_i, 0)

    def back(fh, dx, y, first=False):
        jj = jat(dx, y)
        ugt[...] = jnp.transpose(ugall[fh, jj].reshape(256, 256).astype(F32)).astype(BF16)
        for zs in range(8):
            part = jnp.dot(
                ugt[...],
                amat[pl.ds(pl.multiple_of(jj * 256, 256), 256), zs * 256 : zs * 256 + 256],
                preferred_element_type=F32,
            )
            acc2[fh, zs] = part if first else acc2[fh, zs] + part

        @pl.when(j // 4 == fh)
        def _():
            ug_out[:, pl.ds(pl.multiple_of(jj * 256, 256), 256)] = ugt[
                pl.ds(pl.multiple_of((j % 4) * 64, 64), 64), :
            ]

    def piece(fh, zs, y, cc):
        v = acc2[fh, :, pl.ds(pl.multiple_of((zs * 4 + y * 2 + cc) * 8, 8), 8), :]
        return jnp.concatenate([v[0:4], v[4:8]], axis=1)

    def core_start(fh):
        for d in (4, 3, -3, 1, -1, 2, -2, 0):
            zs = (z + d + 8) % 8
            for y in range(2):
                cs[fh, zs, y] = piece(fh, zs, y, 1 - c).astype(BF16)
            send(cs.at[fh, zs], cr.at[fh, zs], sem_ucs.at[fh, d % 8], sem_ucr.at[fh, d % 8], core)

    def core_recv(fh, d):
        recv(cr.at[fh, (z + d + 8) % 8], sem_ucs.at[fh, d % 8], sem_ucr.at[fh, d % 8], core)

    def own_sum(fh, d, y):
        zs = (z + d + 8) % 8
        return piece(fh, zs, y, c) + cr[fh, zs, y].astype(F32)

    def z_send(fh, d, k, slot, value, dist):
        n = (fh, d, k, slot)
        rs[n] = value.astype(BF16)
        dev = at_zy(DIR[d] * dist) if k == 0 and slot < 2 else at_z(DIR[d] * dist)
        send(rs.at[n], rr.at[n], sem_uzs.at[n], sem_uzr.at[n], dev)

    def z_recv(fh, d, k, slot):
        n = (fh, d, k, slot)
        recv(rr.at[n], sem_uzs.at[n], sem_uzr.at[n], at_z(-DIR[d]))
        return rr[n].astype(F32)

    def uy(k):
        return 1 - yh if k == 0 else yh

    ucombos = [(k, d) for k in range(2) for d in (R, L)]

    def u_out(fh):
        core_recv(fh, 4)
        for k, d in ucombos:
            if hops(d, k) == 4:
                z_send(fh, d, k, 3, own_sum(fh, 4, uy(k)), 2)
        for dist, slot in ((3, 2), (1, 0)):
            core_recv(fh, dist)
            core_recv(fh, -dist)
            for k, d in ucombos:
                z_send(fh, d, k, slot, own_sum(fh, DIR[d] * dist, uy(k)), 1)

    def u_mid(fh):
        core_recv(fh, 2)
        core_recv(fh, -2)
        for k, d in ucombos:
            value = own_sum(fh, DIR[d] * 2, uy(k)) + z_recv(fh, d, k, 2)
            if hops(d, k) == 4:
                value = value + z_recv(fh, d, k, 3)
            z_send(fh, d, k, 1, value, 2)

    def u_cross(fh):
        core_recv(fh, 0)
        ys[fh] = own_sum(fh, 0, 1 - yh).astype(BF16)
        send(ys.at[fh], yr.at[fh], sem_uys.at[fh], sem_uyr.at[fh], y_user)

    def u_final(fh):
        mine = own_sum(fh, 0, yh)
        for k, d in ucombos:
            mine = mine + z_recv(fh, d, k, 0) + z_recv(fh, d, k, 1)
        recv(yr.at[fh], sem_uys.at[fh], sem_uyr.at[fh], y_user)
        return mine + yr[fh].astype(F32)

    def gain_i_wait(k, total):
        remote(gs, gr.at[k], sem_g1s.at[k], sem_g1r.at[k], peer_i(k)).wait()
        return total + gr[k]

    low = lax.broadcasted_iota(jnp.int32, (8, 128), 1) < 64
    top = lax.broadcasted_iota(jnp.int32, (8, 128), 0) < 4
    def all_to_all(src, dst, ssem, rsem):
        def body(k, _):
            remote(src((u + k) % 32), dst.at[u], ssem.at[0], rsem.at[0], peer_u(k)).start()
            return 0

        lax.fori_loop(1, 32, body, 0)

    def all_arrived(dst, ssem, rsem):
        every = dst.at[pl.ds(0, 31)]
        remote(every, every, ssem.at[0], rsem.at[0], core).wait()

    back(0, 0, yl, True)
    items.cross()
    back(1, 0, yl, True)
    g_cross(0)
    g_step(0, 0, 1)
    g_step(1, 0, 1)
    back(0, 1, yl)
    back(0, -1, yl)
    items.near(0)
    g_cross(1)
    back(0, 0, 1 - yl)
    back(1, 1, yl)
    g_step(0, 1, 1)
    back(0, 1, 1 - yl)
    g_step(0, 0, 2)
    back(0, 2, yl)
    g_step(1, 0, 2)
    back(0, -1, 1 - yl)
    gt[...] = jnp.where(top, lax.fori_loop(1, 8, gain_i_wait, gs[...]), cats)
    gr2[u] = gt[...]

    all_to_all(lambda t: gt, gr2, sem_g2s, sem_g2r)
    g_step(0, 1, 2)
    back(0, 2, 1 - yl)
    core_start(0)
    back(1, -1, yl)
    back(1, 0, 1 - yl)
    u_out(0)
    items.near(1)
    items.far(0)
    u_cross(0)
    g_step(1, 1, 1)
    back(1, 2, yl)
    back(1, 1, 1 - yl)
    back(1, -1, 1 - yl)
    g_step(1, 1, 2)
    back(1, 2, 1 - yl)
    core_start(1)
    items.far(1)
    u_out(1)
    u_cross(1)
    u_mid(0)
    all_arrived(gr2, sem_g2s, sem_g2r)
    for p in range(16):
        even = jnp.broadcast_to(gr2[p * 2, 4:5, :], (8, 128))
        odd = jnp.broadcast_to(gr2[p * 2 + 1, 4:5, :], (8, 128))
        catl[p] = jnp.where(low, even, odd)
    gr[0] = jnp.sum(gr2[...], axis=0)
    grow = gr[0, pl.ds(j // 2, 1), :]
    gg_out[...] = jnp.where(j % 2 == 0, grow[:, 0:64], grow[:, 64:128])
    u_mid(1)
    for d in range(-3, 5):
        items.settle(d)
    mine = jnp.concatenate(
        [
            jnp.concatenate([value[:, 0:8], value[:, 8:16]], axis=0)
            for value in (u_final(0), u_final(1))
        ],
        axis=1,
    ).astype(BF16)
    for zs in range(8):
        for half in range(2):
            sumb[zs * 2 + half] = mine[zs, :, half * 128 : half * 128 + 128]

    st[u] = sumb[u // 2]

    for p in range(16):
        cat16 = jnp.concatenate([catl[p], catl[p]], axis=0)
        value = sumb[p].astype(F32)
        for expert in range(4):
            ms[expert * 16 : expert * 16 + 16, p * 128 : p * 128 + 128] = jnp.where(
                cat16 == float(expert), value, 0.0
            ).astype(BF16)
    grads = jnp.zeros((64, 512), F32)
    for zs in range(8):
        grads = grads + jnp.dot(
            ms[:, zs * 256 : zs * 256 + 256], xg[zs].reshape(256, 512), preferred_element_type=F32
        )
    wide = jnp.transpose(jnp.concatenate([grads, grads], axis=0)).reshape(32, 2, 8, 128)
    es[...] = jnp.where(low[None], wide[:, 0], wide[:, 1])
    er[u] = es[u]

    all_to_all(lambda t: es.at[t], er, sem_2s, sem_2r)
    all_to_all(lambda t: sumb.at[t // 2], st, sem_1s, sem_1r)
    for copy in sent:
        copy.wait_send()
    all_arrived(st, sem_1s, sem_1r)
    wide = st[...].astype(F32)
    sums = jnp.concatenate([wide[:, 0:8], wide[:, 8:16]], axis=0).reshape(512, 128)
    cat1 = catl[u // 2][0:1, :]
    total = jnp.zeros((512, 128), F32)
    for expert in range(4):
        masked = jnp.where(cat1 == float(expert), sums, 0.0).astype(BF16)
        total = total + jnp.dot(w[expert], masked, preferred_element_type=F32)
    igt[...] = jnp.transpose(total)
    ig_out[...] = igt[pl.ds(pl.multiple_of(c * 64, 64), 64), :].astype(BF16)

    all_arrived(er, sem_2s, sem_2r)
    lane = lax.broadcasted_iota(jnp.int32, (8, 128), 1) // 8
    for expert in range(4):
        for half in range(2):
            for t in range(4):
                line = jnp.zeros((8, 128), F32)
                for k in range(16):
                    shift = k * 8 - half * 64 - expert * 16 - (t // 2) * 8
                    moved = pltpu.roll(er[(t % 2) * 16 + k], shift % 128, 1)
                    line = jnp.where(lane == k, moved, line)
                eg_out[expert, half * 8 : half * 8 + 8, t * 128 : t * 128 + 128] = line


def settle(ug, ig, eg, gg, ug_out, ig_out, eg_out, gg_out):
    for src, dst in ((ug, ug_out), (ig, ig_out), (eg, eg_out), (gg, gg_out)):
        dst[...] = src[...]


def on_device(
    user_feat, cotangent, gain, item_feat, categories, expert_w, tile_place, tile_level, tile_count
):
    vmem = pl.BlockSpec(memory_space=pltpu.VMEM)
    smem = pl.BlockSpec(memory_space=pltpu.SMEM)
    hbm = pl.BlockSpec(memory_space=pl.ANY)
    V = pltpu.VMEM
    scratch = [
        V((8, 4, 64, 512), BF16), V((2, 8, 4, 64, 256), BF16), V((4, 512, 512), BF16), V((80, 128, 128), jnp.int32),
        V((2048, 2048), BF16), V((2, 16, 128, 256), F32),
        V((256, 512), BF16), V((256, 512), BF16), V((16, 8, 128), F32),
        V((8, 128), jnp.int32), pltpu.SMEM((8, 128), jnp.int32),
        V((2, 2, 2, 2, 2, 128, 256), BF16), V((2, 2, 2, 2, 2, 128, 256), BF16),
        V((5, 2, 128, 256), BF16), V((5, 2, 128, 256), BF16),
        V((2, 8, 2, 128, 256), BF16), V((256, 256), BF16), V((2, 8, 256, 256), F32),
        V((2, 8, 2, 4, 16, 256), BF16), V((2, 8, 2, 4, 16, 256), BF16),
        V((2, 2, 2, 4, 4, 16, 256), BF16), V((2, 2, 2, 4, 4, 16, 256), BF16),
        V((2, 4, 16, 256), BF16), V((2, 4, 16, 256), BF16),
        V((16, 16, 128), BF16), V((32, 16, 128), BF16), V((64, 2048), BF16),
        V((32, 8, 128), F32), V((32, 8, 128), F32), V((128, 512), F32),
        V((8, 128), F32), V((8, 8, 128), F32), V((8, 128), F32), V((32, 8, 128), F32),
        DMA((5,)), DMA((2, 2, 33)), DMA((2, 33)),
        DMA((2, 2, 2, 2, 2)), DMA((2, 2, 2, 2, 2)), DMA((5, 2)), DMA((5, 2)),
        DMA((2, 2, 2, 2, 2)), DMA((2, 2, 2, 2, 2)), DMA((2, 2)), DMA((2, 2)),
        DMA((2, 8)), DMA((2, 8)), DMA((2, 2, 2, 4)), DMA((2, 2, 2, 4)), DMA((2,)), DMA((2,)),
        DMA((1,)), DMA((1,)), DMA((1,)), DMA((1,)), DMA((8,)), DMA((8,)), DMA((1,)), DMA((1,)),
    ]
    shapes = (
        jax.ShapeDtypeStruct((64, 2048), BF16),
        jax.ShapeDtypeStruct((64, 512), BF16),
        jax.ShapeDtypeStruct((4, 16, 512), F32),
        jax.ShapeDtypeStruct((1, 64), F32),
    )
    parts = pl.pallas_call(
        layer,
        out_shape=shapes,
        in_specs=[vmem, vmem, vmem, smem, smem, hbm, hbm, hbm, hbm],
        out_specs=(vmem, vmem, vmem, vmem),
        scratch_shapes=scratch,
        compiler_params=pltpu.CompilerParams(
            collective_id=0, has_side_effects=True, vmem_limit_bytes=60 * 2**20
        ),
    )(
        item_feat[0], categories, gain[None, :], tile_place[0, 0], tile_count, expert_w, tile_level[0, 0],
        user_feat, cotangent,
    )
    ug, ig, eg, gg = pl.pallas_call(
        settle,
        out_shape=shapes,
        in_specs=[vmem] * 4,
        out_specs=(vmem,) * 4,
    )(*parts)
    return ug.T, ig[None], eg, gg[0]


def solution(mesh):
    placed = (
        P("user", None),
        P("user", None),
        P(),
        P("item", "user", None),
        P("item", "user"),
        P("item", None, None),
        P("user", "item", None),
        P("user", "item", None, None, None),
        P("user", "item"),
    )
    return jax.shard_map(
        on_device,
        mesh=mesh,
        in_specs=placed,
        out_specs=(P("user", "item"), P("item", "user", None), P("item", "user", None), P("item")),
        check_vma=False,
    )
```
